32 devices in a mesh: rep: 1, seq: 8 (over z, y), head: 2 (over x), sub: 2 (over core).
Axes of the slice: x: 2, y: 2, z: 4, core: 2. Of those that a mesh axis runs over, the one named last changes fastest.
Arguments:
- head_query_rows: bfloat16 [2048, 2048], P(('rep', 'seq', 'sub'), 'head'), may hold values from -6 to 6, as said below
- head_key_rows: bfloat16 [2048, 2048], P(('rep', 'seq', 'sub'), 'head'), may hold values from -6 to 6, as said below
- head_value_rows: bfloat16 [2048, 2048], P(('rep', 'seq', 'sub'), 'head'), may hold values from -6 to 6
- output_gradient: bfloat16 [2048, 4096], P(('rep', 'seq', 'sub'), 'head'), may hold values from -6 to 6
- output_matrix: bfloat16 [2048, 4096], P('head', 'sub'), may hold values from -0.125 to 0.125
- adapter_down_weight: bfloat16 [2048, 16], P('head'), may hold values from -0.125 to 0.125
- adapter_up_weight: bfloat16 [16, 4096], replicated, may hold values from -0.09375 to 0.09375
Outputs:
- query_gradient: bfloat16 [2048, 2048], P(('rep', 'seq', 'sub'), 'head')
- key_gradient: bfloat16 [2048, 2048], P(('rep', 'seq', 'sub'), 'head')
- value_gradient: bfloat16 [2048, 2048], P(('rep', 'seq', 'sub'), 'head')
- adapter_down_gradient: float32 [2048, 16], P(('rep', 'head'))
- adapter_up_gradient: float32 [16, 4096], P('rep', 'head')
The draws below stay inside these ranges and needn't reach their ends.
Inputs may be any that keep to these rules, and one draw needn't show every extreme that they name: `head_query_rows`: entries of the queries are real values within the range. `head_key_rows`: entries of the keys are real values within the range.
All inputs are finite; a program needn't handle non-finite values.
Results may differ from the reference program's by a relative error of at most 0.029.
Values may be sent and summed in bfloat16 or wider, within the bound.
A program may use at most 64 MiB of HBM per device.

```python
import jax
import jax.numpy as jnp
from jax import lax

HD = 128
HEADS = 16
MODEL_WIDTH = 4096
LOW_RANK = 16
GROUP = 2048
TOK_DEV = 128
SEQ = 2048
HEAD_FEATURES = 2048


def paired_rows(key):
    base = jax.random.fold_in(key, 11)
    streams = jax.random.split(base, 2)
    shape = (SEQ, HEAD_FEATURES)
    query_raw = jnp.clip(jax.random.normal(streams[0], shape, jnp.float32), -6.0, 6.0)
    key_raw = jnp.clip(jax.random.normal(streams[1], shape, jnp.float32), -6.0, 6.0)
    return (query_raw, key_raw)


def draw_head_query_rows(key, part):
    return paired_rows(key)[0].astype(jnp.bfloat16)


def draw_head_key_rows(key, part):
    return paired_rows(key)[1].astype(jnp.bfloat16)


def level_of(stream_key, extent, cuts, least, largest):
    gain, own = 1.0, jax.random.fold_in(stream_key, 6)
    for dim, blocks in cuts:
        steps = jnp.exp(jax.random.uniform(jax.random.fold_in(own, dim), (blocks,), jnp.float32, least / len(cuts), largest / len(cuts)))
        gain = gain * jnp.repeat(steps, extent[dim] // blocks).reshape([-1 if axis == dim else 1 for axis in range(len(extent))])
    return gain


def noise(rng, extent, spread, limit, cuts=(), held_as=jnp.bfloat16):
    entries = jax.random.normal(rng, extent, jnp.float32) * spread
    if len(cuts) > 0:
        entries = level_of(rng, extent, cuts, -0.22, 0.18) * entries
    return jnp.clip(entries, min=-limit, max=limit).astype(held_as)


def setup_inputs(seed: int = 0, part: int = 0) -> dict:
    streams_of = jax.random.split(jax.random.key(seed), 8)
    part_splits = jax.random.split(jax.random.fold_in(streams_of[7], part), 8)
    return {
        "head_query_rows": draw_head_query_rows(jax.random.fold_in(jax.random.fold_in(streams_of[7], part), 71), part),
        "head_key_rows": draw_head_key_rows(jax.random.fold_in(jax.random.fold_in(streams_of[7], part), 71), part),
        "head_value_rows": noise(part_splits[2], (SEQ, HEAD_FEATURES), 1.0, 6.0, ((0, 16), (1, 2))),
        "output_gradient": noise(part_splits[3], (SEQ, MODEL_WIDTH), 1.0, 6.0, ((0, 16), (1, 2))),
        "output_matrix": noise(streams_of[4], (HEAD_FEATURES, MODEL_WIDTH), HEAD_FEATURES ** -0.5, 0.125, ((0, 2), (1, 2))),
        "adapter_down_weight": noise(streams_of[5], (HEAD_FEATURES, LOW_RANK), HEAD_FEATURES ** -0.5, 0.125, ((0, 2),)),
        "adapter_up_weight": noise(streams_of[6], (LOW_RANK, MODEL_WIDTH), MODEL_WIDTH ** -0.5, 0.09375),
    }


def exact_dot(left, right):
    return jnp.dot(left.astype(jnp.float32), right.astype(jnp.float32), precision=lax.Precision.HIGHEST)


def group_pass(pieces):
    query_g, key_g, value_g, dout_g = pieces
    inverse = HD ** -0.5
    row_idx = lax.broadcasted_iota(jnp.int32, (GROUP, GROUP), 0)
    col_idx = lax.broadcasted_iota(jnp.int32, (GROUP, GROUP), 1)
    visible = col_idx <= row_idx
    scores = exact_dot(query_g, key_g.T) * inverse
    scores = jnp.where(visible, scores, -jnp.inf)
    highest = jnp.max(scores, axis=1, keepdims=True)
    powers = jnp.exp(scores - highest)
    prob = powers / jnp.sum(powers, axis=1, keepdims=True)
    prob_lo = prob.astype(jnp.bfloat16)
    attn_g = exact_dot(prob_lo, value_g).astype(jnp.bfloat16)
    dprob = exact_dot(dout_g, value_g.T)
    delta = jnp.sum(prob * dprob, axis=1, keepdims=True)
    dscore = (prob * (dprob - delta) * inverse).astype(jnp.bfloat16)
    grad_q = exact_dot(dscore, key_g).astype(jnp.bfloat16)
    blocks = GROUP // TOK_DEV
    score_grad_blocks = dscore.reshape(blocks, TOK_DEV, GROUP).astype(jnp.float32)
    query_tiles = query_g.reshape(blocks, TOK_DEV, HD).astype(jnp.float32)
    key_partials = jnp.einsum("srz,srj->szj", score_grad_blocks, query_tiles, precision=lax.Precision.HIGHEST)
    key_partials = lax.optimization_barrier(key_partials.astype(jnp.bfloat16)).astype(jnp.float32)
    grad_k = jnp.sum(key_partials, axis=0).astype(jnp.bfloat16)
    probability_blocks = prob_lo.reshape(blocks, TOK_DEV, GROUP).astype(jnp.float32)
    output_grad_blocks = dout_g.reshape(blocks, TOK_DEV, HD).astype(jnp.float32)
    value_partials = jnp.einsum("srz,srj->szj", probability_blocks, output_grad_blocks, precision=lax.Precision.HIGHEST)
    value_partials = lax.optimization_barrier(value_partials.astype(jnp.bfloat16)).astype(jnp.float32)
    grad_v = jnp.sum(value_partials, axis=0).astype(jnp.bfloat16)
    return attn_g, grad_q, grad_k, grad_v


def heads_pass(query_h, key_h, value_h, dout_h, roll_by):
    count = query_h.shape[0]

    def prepare(tensor):
        return jnp.roll(tensor, -roll_by, axis=1).reshape(count * (SEQ // GROUP), GROUP, HD)

    results = lax.map(group_pass, (prepare(query_h), prepare(key_h), prepare(value_h), prepare(dout_h)))

    def restore(tensor):
        return jnp.roll(tensor.reshape(count, SEQ, HD), roll_by, axis=1)

    return tuple(restore(result) for result in results)


def split_heads(tensor):
    return tensor.reshape(SEQ, HEADS, HD).transpose(1, 0, 2)


def join_heads(tensor):
    return tensor.transpose(1, 0, 2).reshape(SEQ, HEAD_FEATURES)


def reference(head_query_rows, head_key_rows, head_value_rows, output_gradient, output_matrix, adapter_down_weight, adapter_up_weight):
    adapter_upward = exact_dot(output_gradient, adapter_up_weight.T)
    projected_output = exact_dot(output_gradient, output_matrix.T)
    adapter_backward = exact_dot(adapter_upward, adapter_down_weight.T)
    attention_gradient = (projected_output + 2.0 * adapter_backward).astype(jnp.bfloat16)
    per_head = [split_heads(tensor) for tensor in (head_query_rows, head_key_rows, head_value_rows, attention_gradient)]
    half_heads = HEADS // 2
    plain_heads = heads_pass(*[tensor[:half_heads] for tensor in per_head], 0)
    moved_heads = heads_pass(*[tensor[half_heads:] for tensor in per_head], GROUP // 2)
    joined = [join_heads(jnp.concatenate((first, second), axis=0)) for first, second in zip(plain_heads, moved_heads)]
    attention_output, query_gradient, key_gradient, value_gradient = joined
    adapter_middle = exact_dot(attention_output, adapter_down_weight)
    adapter_down_gradient = 2.0 * exact_dot(attention_output.T, adapter_upward)
    adapter_up_gradient = 2.0 * exact_dot(adapter_middle.T, output_gradient)
    return query_gradient, key_gradient, value_gradient, adapter_down_gradient, adapter_up_gradient
```

```python
import jax
import jax.numpy as jnp
from jax import lax
from jax.experimental import pallas as pl
from jax.experimental.pallas import tpu as pltpu
from jax.sharding import PartitionSpec as P

HD = 128
GROUP = 2048


def passed_along(value, axis, by):
    peers = lax.axis_size(axis)
    return lax.ppermute(value, axis, [(i, (i + by) % peers) for i in range(peers)])


def placed_visible(row_count, window_rows, seq_total, first_row, back_rows, roll_by):
    query_pos = first_row + lax.broadcasted_iota(jnp.int32, (row_count, window_rows), 0)
    key_pos = (
        first_row
        - back_rows
        + seq_total
        + lax.broadcasted_iota(jnp.int32, (row_count, window_rows), 1)
    ) % seq_total
    query_order = (query_pos - roll_by + seq_total) % seq_total
    key_order = (key_pos - roll_by + seq_total) % seq_total
    return (query_order // GROUP == key_order // GROUP) & (key_order <= query_order)


def softmax_rows(query_head, keys_head, visible):
    scores = lax.dot_general(
        query_head, keys_head, (((1,), (1,)), ((), ())), preferred_element_type=jnp.float32
    )
    scores = jnp.where(visible, scores * HD ** (-0.5), -jnp.inf)
    highest = jnp.max(scores, axis=1, keepdims=True)
    powers = jnp.exp(scores - highest)
    return powers / jnp.sum(powers, axis=1, keepdims=True)


def head_forward(query_head, window_head, visible):
    prob = softmax_rows(query_head, window_head[0], visible)
    return jnp.dot(
        prob.astype(jnp.bfloat16), window_head[1], preferred_element_type=jnp.float32
    ).astype(jnp.bfloat16)


def head_backward(query_head, window_head, dout_head, visible):
    prob = softmax_rows(query_head, window_head[0], visible)
    prob_lo = prob.astype(jnp.bfloat16)
    dprob = lax.dot_general(
        dout_head, window_head[1], (((1,), (1,)), ((), ())), preferred_element_type=jnp.float32
    )
    delta = jnp.sum(prob * dprob, axis=1, keepdims=True)
    dscore = (prob * (dprob - delta) * HD ** (-0.5)).astype(jnp.bfloat16)
    grad_q = jnp.dot(dscore, window_head[0], preferred_element_type=jnp.float32).astype(
        jnp.bfloat16
    )
    grad_k = lax.dot_general(
        dscore, query_head, (((0,), (0,)), ((), ())), preferred_element_type=jnp.float32
    )
    grad_v = lax.dot_general(
        prob_lo, dout_head, (((0,), (0,)), ((), ())), preferred_element_type=jnp.float32
    )
    return (grad_q, jnp.stack((grad_k.astype(jnp.bfloat16), grad_v.astype(jnp.bfloat16))))


def attend_window(query_rows, window, dout_rows, visible):
    row_count, feat_count = query_rows.shape
    heads_here = feat_count // HD
    window_rows = window.shape[1]
    window_heads = window.reshape(2, window_rows, heads_here, HD).transpose(2, 0, 1, 3)
    query_heads = query_rows.reshape(row_count, heads_here, HD).transpose(1, 0, 2)
    dout_heads = dout_rows.reshape(row_count, heads_here, HD).transpose(1, 0, 2)
    attn_heads = lax.map(
        lambda pieces: head_forward(pieces[0], pieces[1], visible), (query_heads, window_heads)
    )
    grad_q_heads, pair_heads = lax.map(
        lambda pieces: head_backward(pieces[0], pieces[1], pieces[2], visible),
        (query_heads, window_heads, dout_heads),
    )
    attention_output = attn_heads.transpose(1, 0, 2).reshape(row_count, feat_count)
    query_gradient = grad_q_heads.transpose(1, 0, 2).reshape(row_count, feat_count)
    pair_grads = pair_heads.transpose(1, 2, 0, 3).reshape(2, window_rows, feat_count)
    return (attention_output, query_gradient, pair_grads)


def on_device_windows(
    head_query_rows,
    head_key_rows,
    head_value_rows,
    output_gradient,
    output_matrix,
    adapter_down_weight,
    adapter_up_weight,
):
    tokens_dev, feat_dev = head_query_rows.shape
    head_index = lax.axis_index("head")
    shifted = head_index >= lax.axis_size("head") // 2
    total_gradient = lax.all_gather(output_gradient, "head", axis=1, tiled=True)
    projected_output = lax.dot_general(
        total_gradient,
        lax.all_gather(output_matrix, "sub", axis=1, tiled=True),
        (((1,), (1,)), ((), ())),
        preferred_element_type=jnp.float32,
    )
    adapter_upward = lax.dot_general(
        total_gradient,
        adapter_up_weight,
        (((1,), (1,)), ((), ())),
        preferred_element_type=jnp.float32,
    )
    adapter_backward = jnp.dot(
        adapter_upward, adapter_down_weight.astype(jnp.float32).T, precision=lax.Precision.HIGHEST
    )
    attention_gradient = (projected_output + 2.0 * adapter_backward).astype(jnp.bfloat16)
    sub_count = lax.axis_size("sub")
    block_rows = tokens_dev * sub_count
    seq_total = block_rows * lax.axis_size("seq")
    reach = max(GROUP // block_rows - 1, 1)
    roll_by = jnp.where(shifted, GROUP // 2, 0)
    stacked = jnp.stack((head_query_rows, head_key_rows, head_value_rows, attention_gradient))
    moved = lax.all_to_all(stacked, "sub", split_axis=2, concat_axis=1, tiled=True)
    own_pair = moved[1:3]
    received = [passed_along(own_pair, "seq", distance) for distance in range(reach, 0, -1)]
    window = jnp.concatenate(received + [own_pair], axis=1)
    first_row = lax.axis_index("seq") * block_rows
    visible = placed_visible(
        block_rows, window.shape[1], seq_total, first_row, reach * block_rows, roll_by
    )
    attn_local, grad_q_local, pair_grads = attend_window(moved[0], window, moved[3], visible)
    running = pair_grads[:, reach * block_rows :].astype(jnp.float32)
    for distance in range(1, reach + 1):
        begin_row = (reach - distance) * block_rows
        block_terms = pair_grads[:, begin_row : begin_row + block_rows]
        returned = passed_along(block_terms, "seq", -distance)
        running = running + returned.astype(jnp.float32)
    pair_local = running.astype(jnp.bfloat16)
    back = jnp.stack((attn_local, grad_q_local, pair_local[0], pair_local[1]))
    restored = lax.all_to_all(back, "sub", split_axis=1, concat_axis=2, tiled=True)
    attention_output = restored[0]
    query_gradient = restored[1]
    key_gradient = restored[2]
    value_gradient = restored[3]
    middle_piece = jnp.dot(
        attention_output, adapter_down_weight, preferred_element_type=jnp.float32
    )
    down_gradient_part = 2.0 * jnp.dot(
        attention_output.astype(jnp.float32).T, adapter_upward, precision=lax.Precision.HIGHEST
    )
    adapter_middle = lax.psum(middle_piece, "head")
    up_gradient_part = 2.0 * jnp.dot(
        adapter_middle.T, output_gradient.astype(jnp.float32), precision=lax.Precision.HIGHEST
    )
    adapter_down_gradient, adapter_up_gradient = lax.psum(
        (down_gradient_part, up_gradient_part), ("seq", "sub")
    )
    return (
        query_gradient,
        key_gradient,
        value_gradient,
        adapter_down_gradient,
        adapter_up_gradient,
    )


SCALE = HD ** (-0.5)
F32, BF16 = jnp.float32, jnp.bfloat16


def dot_nn(left, right):
    return lax.dot_general(left, right, (((1,), (0,)), ((), ())), preferred_element_type=F32)


def dot_nt(left, right):
    return lax.dot_general(left, right, (((1,), (1,)), ((), ())), preferred_element_type=F32)


def swapped(value, axis):
    return lax.ppermute(value, axis, [(0, 1), (1, 0)])


def attention_kernel(
    blocks, place_ref, own_ref, other_ref, dout_ref, attn_ref, dq_ref, mine_ref, theirs_ref,
    queries, keys, values, douts, keys_t, values_t, dkeys, dvalues,
):
    half = HD
    sub, first = place_ref[0], place_ref[1]
    own_at = sub * half
    other_at = half - own_at

    def gather(o, carry):
        b = lax.rem(o + first, blocks)
        at = pl.multiple_of(o * 2 * half, half)
        queries[pl.ds(pl.multiple_of(o * half, half), half), :] = own_ref[b, 0]
        douts[pl.ds(pl.multiple_of(o * half, half), half), :] = dout_ref[b]
        keys[pl.ds(pl.multiple_of(at + own_at, half), half), :] = own_ref[b, 1]
        values[pl.ds(pl.multiple_of(at + own_at, half), half), :] = own_ref[b, 2]
        keys[pl.ds(pl.multiple_of(at + other_at, half), half), :] = other_ref[b, 0]
        values[pl.ds(pl.multiple_of(at + other_at, half), half), :] = other_ref[b, 1]
        return carry

    lax.fori_loop(0, blocks, gather, 0)
    keys_t[...] = keys[...].T
    values_t[...] = values[...].T
    tile = 2 * half
    tiles = blocks // 2
    for u in reversed(range(tiles)):
        extent = (u + 1) * 2 * tile
        settled = extent - 2 * tile
        q = queries[u * tile : (u + 1) * tile, :]
        g = douts[u * tile : (u + 1) * tile, :]
        scores = dot_nt(keys[:extent, :], q) * SCALE
        key_at = lax.broadcasted_iota(jnp.int32, (2 * tile, tile), 0)
        row = lax.broadcasted_iota(jnp.int32, (2 * tile, tile), 1)
        query_at = row + jnp.where(row >= half, half, 0) + own_at
        edge = jnp.where(key_at <= query_at, scores[settled:, :], -jnp.inf)
        scores = edge if settled == 0 else jnp.concatenate((scores[:settled, :], edge), axis=0)
        powers = jnp.exp(scores - jnp.max(scores, axis=0, keepdims=True))
        prob = powers * (1.0 / jnp.sum(powers, axis=0, keepdims=True))
        prob_lo = prob.astype(BF16)
        attn = dot_nn(values_t[:, :extent], prob_lo).T.astype(BF16)
        dprob = dot_nt(values[:extent, :], g)
        delta = jnp.sum(prob * dprob, axis=0, keepdims=True)
        dscore = (prob * (dprob - delta) * SCALE).astype(BF16)
        dq = dot_nn(keys_t[:, :extent], dscore).T.astype(BF16)
        dk = dot_nn(dscore, q)
        dv = dot_nn(prob_lo, g)
        if u == tiles - 1:
            dkeys[:extent, :] = dk
            dvalues[:extent, :] = dv
        else:
            dkeys[:extent, :] += dk
            dvalues[:extent, :] += dv
        for part in range(2):
            b = lax.rem(2 * u + part + first, blocks)
            attn_ref[b] = attn[part * half : (part + 1) * half, :]
            dq_ref[b] = dq[part * half : (part + 1) * half, :]

    def scatter(o, carry):
        b = lax.rem(o + first, blocks)
        at = pl.multiple_of(o * 2 * half, half)
        own = pl.ds(pl.multiple_of(at + own_at, half), half)
        other = pl.ds(pl.multiple_of(at + other_at, half), half)
        mine_ref[b, 0] = dkeys[own, :]
        mine_ref[b, 1] = dvalues[own, :]
        theirs_ref[b, 0] = dkeys[other, :].astype(BF16)
        theirs_ref[b, 1] = dvalues[other, :].astype(BF16)
        return carry

    lax.fori_loop(0, blocks, scatter, 0)


def attention(place, own, other, dout):
    blocks = own.shape[0]
    rows = own.shape[2]
    total = 2 * blocks * rows
    vmem = pl.BlockSpec(memory_space=pltpu.VMEM)
    return pl.pallas_call(
        lambda *refs: attention_kernel(blocks, *refs),
        out_shape=(
            jax.ShapeDtypeStruct((blocks, rows, HD), BF16),
            jax.ShapeDtypeStruct((blocks, rows, HD), BF16),
            jax.ShapeDtypeStruct((blocks, 2, rows, HD), F32),
            jax.ShapeDtypeStruct((blocks, 2, rows, HD), BF16),
        ),
        in_specs=[pl.BlockSpec(memory_space=pltpu.SMEM), vmem, vmem, vmem],
        out_specs=[vmem] * 4,
        scratch_shapes=[
            pltpu.VMEM((total // 2, HD), BF16),
            pltpu.VMEM((total, HD), BF16),
            pltpu.VMEM((total, HD), BF16),
            pltpu.VMEM((total // 2, HD), BF16),
            pltpu.VMEM((HD, total), BF16),
            pltpu.VMEM((HD, total), BF16),
            pltpu.VMEM((total, HD), F32),
            pltpu.VMEM((total, HD), F32),
        ],
        compiler_params=pltpu.CompilerParams(vmem_limit_bytes=48 * 1024 * 1024),
        cost_estimate=pl.CostEstimate(
            flops=12 * total * total // 4 * HD, bytes_accessed=20 * total * HD, transcendentals=0
        ),
    )(place, own, other, dout)


def by_head(value, heads):
    rows = value.shape[0]
    return value.reshape(rows, heads, HD).transpose(1, 0, 2)


def exact(left, right):
    return jnp.dot(left, right, preferred_element_type=F32, precision=lax.Precision.HIGHEST)


def on_device_heads(
    head_query_rows,
    head_key_rows,
    head_value_rows,
    output_gradient,
    output_matrix,
    adapter_down_weight,
    adapter_up_weight,
):
    rows, feats = head_query_rows.shape
    heads = feats // HD
    cols = output_gradient.shape[1]
    head, sub = lax.axis_index("head"), lax.axis_index("sub")
    gradient_away = swapped(output_gradient, "head")
    matrix_away = swapped(output_matrix, "sub")
    projections = jnp.stack(
        (by_head(head_query_rows, heads), by_head(head_key_rows, heads), by_head(head_value_rows, heads)),
        axis=1,
    )
    own = lax.all_to_all(projections, "seq", split_axis=0, concat_axis=0, tiled=True)
    other = swapped(own[:, 1:], "sub")
    same = head == sub
    projected = dot_nt(jnp.where(same, output_gradient, gradient_away), output_matrix) + dot_nt(
        jnp.where(same, gradient_away, output_gradient), matrix_away
    )
    up_here = lax.dynamic_slice_in_dim(adapter_up_weight, head * cols, cols, axis=1)
    up_away = lax.dynamic_slice_in_dim(adapter_up_weight, (1 - head) * cols, cols, axis=1)
    adapter_upward = dot_nt(output_gradient, up_here) + dot_nt(gradient_away, up_away)
    adapter_backward = exact(adapter_upward, adapter_down_weight.astype(F32).T)
    dout = (projected + 2.0 * adapter_backward).astype(BF16)
    dout = lax.all_to_all(by_head(dout, heads), "seq", split_axis=0, concat_axis=0, tiled=True)
    shifted = head >= lax.axis_size("head") // 2
    place = jnp.stack((sub, jnp.where(shifted, GROUP // 2 // (2 * rows), 0))).astype(jnp.int32)
    attn, dq, mine, theirs = attention(place, own, other, dout)
    pair = (mine + swapped(theirs, "sub").astype(F32)).astype(BF16)
    back = jnp.concatenate((attn[:, None], dq[:, None], pair), axis=1)
    back = lax.all_to_all(back, "seq", split_axis=0, concat_axis=0, tiled=True)
    attn, dq, dk, dv = [back[:, n].transpose(1, 0, 2).reshape(rows, feats) for n in range(4)]
    middle_part = jnp.dot(attn, adapter_down_weight, preferred_element_type=F32)
    middle = middle_part + swapped(middle_part, "head")
    rank = middle.shape[1]
    down_part = 2.0 * exact(adapter_upward.T, attn.astype(F32))
    up_part = 2.0 * exact(middle.T, output_gradient.astype(F32))
    parts = jnp.concatenate((down_part, up_part), axis=1)
    peers = 2 * heads
    width = parts.shape[1] // peers
    parts = parts.reshape(rank, peers, width).transpose(1, 0, 2)
    terms = lax.all_to_all(parts, ("seq", "sub"), split_axis=0, concat_axis=0, tiled=True)
    piece = jnp.sum(terms, axis=0)
    spread = jnp.broadcast_to(piece[None], (peers, rank, width))
    whole = lax.all_to_all(spread, ("seq", "sub"), split_axis=0, concat_axis=0, tiled=True)
    whole = whole.transpose(1, 0, 2).reshape(rank, peers * width)
    return dq, dk, dv, whole[:, :feats].T, whole[:, feats:]


def one_group(mesh, rows, feats, width):
    seq, head, sub = mesh.shape["seq"], mesh.shape["head"], mesh.shape["sub"]
    return (
        sub == 2
        and head == 2
        and rows == HD
        and seq % 2 == 0
        and seq * sub * rows == GROUP
        and feats == seq * HD
        and (feats + width) % (seq * sub) == 0
    )


def solution(mesh):
    in_specs = (
        P(("rep", "seq", "sub"), "head"),
        P(("rep", "seq", "sub"), "head"),
        P(("rep", "seq", "sub"), "head"),
        P(("rep", "seq", "sub"), "head"),
        P("head", "sub"),
        P("head", None),
        P(),
    )
    out_specs = (
        P(("rep", "seq", "sub"), "head"),
        P(("rep", "seq", "sub"), "head"),
        P(("rep", "seq", "sub"), "head"),
        P(("rep", "head"), None),
        P("rep", "head"),
    )

    def on_device(*local):
        if one_group(mesh, *local[0].shape, local[3].shape[1]):
            return on_device_heads(*local)
        return on_device_windows(*local)

    return jax.shard_map(
        on_device, mesh=mesh, in_specs=in_specs, out_specs=out_specs, check_vma=False
    )
```

```python
import jax
import jax.numpy as jnp
from jax import lax
from jax.experimental import pallas as pl
from jax.experimental.pallas import tpu as pltpu
from jax.sharding import PartitionSpec as P

HD = 128
GROUP = 2048


def passed_along(value, axis, by):
    peers = lax.axis_size(axis)
    return lax.ppermute(value, axis, [(i, (i + by) % peers) for i in range(peers)])


def placed_visible(row_count, window_rows, seq_total, first_row, back_rows, roll_by):
    query_pos = first_row + lax.broadcasted_iota(jnp.int32, (row_count, window_rows), 0)
    key_pos = (
        first_row
        - back_rows
        + seq_total
        + lax.broadcasted_iota(jnp.int32, (row_count, window_rows), 1)
    ) % seq_total
    query_order = (query_pos - roll_by + seq_total) % seq_total
    key_order = (key_pos - roll_by + seq_total) % seq_total
    return (query_order // GROUP == key_order // GROUP) & (key_order <= query_order)


def softmax_rows(query_head, keys_head, visible):
    scores = lax.dot_general(
        query_head, keys_head, (((1,), (1,)), ((), ())), preferred_element_type=jnp.float32
    )
    scores = jnp.where(visible, scores * HD ** (-0.5), -jnp.inf)
    highest = jnp.max(scores, axis=1, keepdims=True)
    powers = jnp.exp(scores - highest)
    return powers / jnp.sum(powers, axis=1, keepdims=True)


def head_forward(query_head, window_head, visible):
    prob = softmax_rows(query_head, window_head[0], visible)
    return jnp.dot(
        prob.astype(jnp.bfloat16), window_head[1], preferred_element_type=jnp.float32
    ).astype(jnp.bfloat16)


def head_backward(query_head, window_head, dout_head, visible):
    prob = softmax_rows(query_head, window_head[0], visible)
    prob_lo = prob.astype(jnp.bfloat16)
    dprob = lax.dot_general(
        dout_head, window_head[1], (((1,), (1,)), ((), ())), preferred_element_type=jnp.float32
    )
    delta = jnp.sum(prob * dprob, axis=1, keepdims=True)
    dscore = (prob * (dprob - delta) * HD ** (-0.5)).astype(jnp.bfloat16)
    grad_q = jnp.dot(dscore, window_head[0], preferred_element_type=jnp.float32).astype(
        jnp.bfloat16
    )
    grad_k = lax.dot_general(
        dscore, query_head, (((0,), (0,)), ((), ())), preferred_element_type=jnp.float32
    )
    grad_v = lax.dot_general(
        prob_lo, dout_head, (((0,), (0,)), ((), ())), preferred_element_type=jnp.float32
    )
    return (grad_q, jnp.stack((grad_k.astype(jnp.bfloat16), grad_v.astype(jnp.bfloat16))))


def attend_window(query_rows, window, dout_rows, visible):
    row_count, feat_count = query_rows.shape
    heads_here = feat_count // HD
    window_rows = window.shape[1]
    window_heads = window.reshape(2, window_rows, heads_here, HD).transpose(2, 0, 1, 3)
    query_heads = query_rows.reshape(row_count, heads_here, HD).transpose(1, 0, 2)
    dout_heads = dout_rows.reshape(row_count, heads_here, HD).transpose(1, 0, 2)
    attn_heads = lax.map(
        lambda pieces: head_forward(pieces[0], pieces[1], visible), (query_heads, window_heads)
    )
    grad_q_heads, pair_heads = lax.map(
        lambda pieces: head_backward(pieces[0], pieces[1], pieces[2], visible),
        (query_heads, window_heads, dout_heads),
    )
    attention_output = attn_heads.transpose(1, 0, 2).reshape(row_count, feat_count)
    query_gradient = grad_q_heads.transpose(1, 0, 2).reshape(row_count, feat_count)
    pair_grads = pair_heads.transpose(1, 2, 0, 3).reshape(2, window_rows, feat_count)
    return (attention_output, query_gradient, pair_grads)


def on_device_windows(
    head_query_rows,
    head_key_rows,
    head_value_rows,
    output_gradient,
    output_matrix,
    adapter_down_weight,
    adapter_up_weight,
):
    tokens_dev, feat_dev = head_query_rows.shape
    head_index = lax.axis_index("head")
    shifted = head_index >= lax.axis_size("head") // 2
    total_gradient = lax.all_gather(output_gradient, "head", axis=1, tiled=True)
    projected_output = lax.dot_general(
        total_gradient,
        lax.all_gather(output_matrix, "sub", axis=1, tiled=True),
        (((1,), (1,)), ((), ())),
        preferred_element_type=jnp.float32,
    )
    adapter_upward = lax.dot_general(
        total_gradient,
        adapter_up_weight,
        (((1,), (1,)), ((), ())),
        preferred_element_type=jnp.float32,
    )
    adapter_backward = jnp.dot(
        adapter_upward, adapter_down_weight.astype(jnp.float32).T, precision=lax.Precision.HIGHEST
    )
    attention_gradient = (projected_output + 2.0 * adapter_backward).astype(jnp.bfloat16)
    sub_count = lax.axis_size("sub")
    block_rows = tokens_dev * sub_count
    seq_total = block_rows * lax.axis_size("seq")
    reach = max(GROUP // block_rows - 1, 1)
    roll_by = jnp.where(shifted, GROUP // 2, 0)
    stacked = jnp.stack((head_query_rows, head_key_rows, head_value_rows, attention_gradient))
    moved = lax.all_to_all(stacked, "sub", split_axis=2, concat_axis=1, tiled=True)
    own_pair = moved[1:3]
    received = [passed_along(own_pair, "seq", distance) for distance in range(reach, 0, -1)]
    window = jnp.concatenate(received + [own_pair], axis=1)
    first_row = lax.axis_index("seq") * block_rows
    visible = placed_visible(
        block_rows, window.shape[1], seq_total, first_row, reach * block_rows, roll_by
    )
    attn_local, grad_q_local, pair_grads = attend_window(moved[0], window, moved[3], visible)
    running = pair_grads[:, reach * block_rows :].astype(jnp.float32)
    for distance in range(1, reach + 1):
        begin_row = (reach - distance) * block_rows
        block_terms = pair_grads[:, begin_row : begin_row + block_rows]
        returned = passed_along(block_terms, "seq", -distance)
        running = running + returned.astype(jnp.float32)
    pair_local = running.astype(jnp.bfloat16)
    back = jnp.stack((attn_local, grad_q_local, pair_local[0], pair_local[1]))
    restored = lax.all_to_all(back, "sub", split_axis=1, concat_axis=2, tiled=True)
    attention_output = restored[0]
    query_gradient = restored[1]
    key_gradient = restored[2]
    value_gradient = restored[3]
    middle_piece = jnp.dot(
        attention_output, adapter_down_weight, preferred_element_type=jnp.float32
    )
    down_gradient_part = 2.0 * jnp.dot(
        attention_output.astype(jnp.float32).T, adapter_upward, precision=lax.Precision.HIGHEST
    )
    adapter_middle = lax.psum(middle_piece, "head")
    up_gradient_part = 2.0 * jnp.dot(
        adapter_middle.T, output_gradient.astype(jnp.float32), precision=lax.Precision.HIGHEST
    )
    adapter_down_gradient, adapter_up_gradient = lax.psum(
        (down_gradient_part, up_gradient_part), ("seq", "sub")
    )
    return (
        query_gradient,
        key_gradient,
        value_gradient,
        adapter_down_gradient,
        adapter_up_gradient,
    )


SCALE = HD ** (-0.5)
F32, BF16 = jnp.float32, jnp.bfloat16
LOOK, DQ, DK, DV = range(4)


def dot_nn(left, right):
    return lax.dot_general(left, right, (((1,), (0,)), ((), ())), preferred_element_type=F32)


def dot_nt(left, right):
    return lax.dot_general(left, right, (((1,), (1,)), ((), ())), preferred_element_type=F32)


def dot_tn(left, right):
    return lax.dot_general(left, right, (((0,), (0,)), ((), ())), preferred_element_type=F32)


def three_terms(value):
    high = value.astype(BF16)
    rest = value - high.astype(F32)
    mid = rest.astype(BF16)
    low = (rest - mid.astype(F32)).astype(BF16)
    return jnp.concatenate((high, mid, low), axis=0)


def folded(product):
    rank = product.shape[0] // 3
    return product[:rank] + product[rank : 2 * rank] + product[2 * rank :]


def whole_kernel(
    n_seq,
    q_ref, k_ref, v_ref, g_ref, w_ref, down_ref, up_ref,
    dq_ref, dk_ref, dv_ref, down_out, up_out,
    g_all, w_all, queries, keys, values, douts, dout_send,
    keys_t, values_t, probs, attn_send, dq_send, attn_full, dkeys, dvalues,
    pair_send, pair_recv, pair_sum, upward, mid_mine, mid_theirs, pieces, gathered, totals,
    local_sem, swap_send, swap_recv, in_send, in_recv, in_local, kv_send, kv_recv,
    do_send, do_recv, back_send, back_recv, back_local, pair_ssem, pair_rsem,
    rs_send, rs_recv, ag_send, ag_recv,
):
    me, head, sub = lax.axis_index("seq"), lax.axis_index("head"), lax.axis_index("sub")
    rank = down_ref.shape[0]
    feats = down_ref.shape[1]
    cols = g_ref.shape[1]
    peers = 2 * n_seq
    mine = me * 2 + sub
    first = head * (n_seq // 2)
    own_at = sub * HD

    def ring(n):
        return lax.rem(me + n, n_seq)

    def place_of(block):
        return lax.rem(block - first + n_seq, n_seq)

    def rows_of(order, which):
        return pl.ds(pl.multiple_of(order * (2 * HD) + which * HD, HD), HD)

    def own_rows(order):
        return pl.ds(pl.multiple_of(order * HD, HD), HD)

    def lanes(block):
        return pl.ds(pl.multiple_of(block * HD, HD), HD)

    def remote(src, dst, send, recv, device):
        return pltpu.make_async_remote_copy(
            src_ref=src, dst_ref=dst, send_sem=send, recv_sem=recv,
            device_id=device, device_id_type=pl.DeviceIdType.MESH,
        )

    def across(src, dst, send, recv, device):
        return remote(src, dst, send, recv, {"seq": device})

    barrier = pltpu.get_barrier_semaphore()

    def greet(n, carry):
        p = lax.rem(mine + n, peers)
        pl.semaphore_signal(
            barrier, inc=1, device_id={"seq": p // 2, "sub": lax.rem(p, 2)},
            device_id_type=pl.DeviceIdType.MESH,
        )
        return carry

    own_g = pltpu.make_async_copy(g_ref, g_all.at[head], local_sem.at[0])
    own_w = pltpu.make_async_copy(w_ref, w_all.at[sub], local_sem.at[1])
    own_g.start()
    own_w.start()
    lax.fori_loop(1, peers, greet, 0)
    pl.semaphore_signal(
        barrier, inc=1, device_id={"head": 1 - head}, device_id_type=pl.DeviceIdType.MESH
    )
    pl.semaphore_wait(barrier, peers)

    g_swap = remote(g_ref, g_all.at[head], swap_send.at[0], swap_recv.at[0], {"head": 1 - head})
    w_swap = remote(w_ref, w_all.at[sub], swap_send.at[1], swap_recv.at[1], {"sub": 1 - sub})
    g_swap.start()
    w_swap.start()

    o_me = place_of(me)

    def inward(n, carry):
        to = ring(n)
        for t, (src, dst, at) in enumerate(
            (
                (k_ref, keys, rows_of(o_me, sub)),
                (v_ref, values, rows_of(o_me, sub)),
                (q_ref, queries, own_rows(o_me)),
            )
        ):
            across(
                src.at[:, lanes(to)], dst.at[at, :], in_send.at[t, to], in_recv.at[t, me], to
            ).start()
        return carry

    lax.fori_loop(1, n_seq, inward, 0)
    own_in = [
        pltpu.make_async_copy(src.at[:, lanes(me)], dst.at[at, :], in_local.at[t])
        for t, (src, dst, at) in enumerate(
            (
                (k_ref, keys, rows_of(o_me, sub)),
                (v_ref, values, rows_of(o_me, sub)),
                (q_ref, queries, own_rows(o_me)),
            )
        )
    ]
    for copy in own_in:
        copy.start()

    own_g.wait()
    own_w.wait()
    g_swap.wait()
    upward[...] = dot_nt(up_ref[:, :cols], g_all[0]) + dot_nt(up_ref[:, cols:], g_all[1])
    w_swap.wait()
    up_terms = three_terms(upward[...])

    def dout_of(h):
        rows = pl.ds(pl.multiple_of(h * HD, HD), HD)
        projected = dot_nt(g_all[0], w_all[0, rows, :]) + dot_nt(g_all[1], w_all[1, rows, :])
        down = down_ref[:, lanes(h)]
        adapter = dot_tn(up_terms, jnp.concatenate((down, down, down), axis=0))
        return (projected + 2.0 * adapter).astype(BF16)

    def send_dout(n, carry):
        to = ring(n)
        dout_send[to] = dout_of(to)
        across(
            dout_send.at[to], douts.at[own_rows(o_me), :], do_send.at[to], do_recv.at[me], to
        ).start()
        return carry

    lax.fori_loop(1, n_seq, send_dout, 0)
    douts[own_rows(o_me), :] = dout_of(me)

    for copy in own_in:
        copy.wait()

    def kv_copy(t, order):
        dst = keys if t == 0 else values
        at = rows_of(order, sub)
        return remote(
            dst.at[at, :], dst.at[at, :], kv_send.at[t, order], kv_recv.at[t, order],
            {"sub": 1 - sub},
        )

    def in_wait(t, frm):
        dst, at = (
            (keys, rows_of(place_of(frm), sub)),
            (values, rows_of(place_of(frm), sub)),
            (queries, own_rows(place_of(frm))),
        )[t]
        src = (k_ref, v_ref, q_ref)[t]
        return across(src.at[:, lanes(frm)], dst.at[at, :], in_send.at[t, frm], in_recv.at[t, frm], frm)

    kv_copy(0, o_me).start()
    kv_copy(1, o_me).start()

    def hand_on(n, carry):
        frm = ring(n_seq - n)
        for t in range(2):
            in_wait(t, frm).wait_recv()
            kv_copy(t, place_of(frm)).start()
        in_wait(2, frm).wait_recv()
        return carry

    lax.fori_loop(1, n_seq, hand_on, 0)

    def kv_arrived(order, carry):
        for t in range(2):
            dst = keys if t == 0 else values
            at = rows_of(order, 1 - sub)
            remote(
                dst.at[at, :], dst.at[at, :], kv_send.at[t, order], kv_recv.at[t, order],
                {"sub": 1 - sub},
            ).wait_recv()
            kv_copy(t, order).wait_send()
        return carry

    lax.fori_loop(0, n_seq, kv_arrived, 0)
    keys_t[...] = keys[...].T
    values_t[...] = values[...].T

    sinks = (attn_full, dq_ref, dk_ref, dv_ref)

    def give(kind, src, order):
        to = lax.rem(order + first, n_seq)
        dst = sinks[kind].at[:, lanes(me)]

        @pl.when(to == me)
        def _():
            pltpu.make_async_copy(src, dst, back_local.at[kind]).start()

        @pl.when(to != me)
        def _():
            across(src, dst, back_send.at[kind, to], back_recv.at[kind, me], to).start()

    def settle(kind):
        src = attn_send.at[own_rows(0), :]
        pltpu.make_async_copy(src, sinks[kind].at[:, lanes(me)], back_local.at[kind]).wait()

        def one(n, carry):
            peer = ring(n)
            copy = across(
                src, sinks[kind].at[:, lanes(peer)], back_send.at[kind, peer],
                back_recv.at[kind, peer], peer,
            )
            copy.wait_send()
            copy.wait_recv()
            return carry

        lax.fori_loop(1, n_seq, one, 0)

    tile = 2 * HD
    tiles = n_seq // 2

    def span(u):
        return u * (u + 1) * tile, (u + 1) * 2 * tile

    for u in reversed(range(tiles)):
        base, extent = span(u)
        settled = extent - 2 * tile
        q = queries[u * tile : (u + 1) * tile, :]
        scores = dot_nt(keys[:extent, :], q) * SCALE
        key_at = lax.broadcasted_iota(jnp.int32, (2 * tile, tile), 0)
        row = lax.broadcasted_iota(jnp.int32, (2 * tile, tile), 1)
        query_at = row + jnp.where(row >= HD, HD, 0) + own_at
        edge = jnp.where(key_at <= query_at, scores[settled:, :], -jnp.inf)
        scores = edge if settled == 0 else jnp.concatenate((scores[:settled, :], edge), axis=0)
        powers = jnp.exp(scores - jnp.max(scores, axis=0, keepdims=True))
        prob = powers * (1.0 / jnp.sum(powers, axis=0, keepdims=True))
        probs[base : base + extent, :] = prob
        attn = dot_nn(values_t[:, :extent], prob.astype(BF16)).T.astype(BF16)
        attn_send[u * tile : (u + 1) * tile, :] = attn
        for order in (2 * u, 2 * u + 1):
            give(LOOK, attn_send.at[order * HD : (order + 1) * HD, :], order)

    def dout_arrived(n, carry):
        frm = ring(n)
        copy = across(
            dout_send.at[frm], douts.at[own_rows(place_of(frm)), :], do_send.at[frm],
            do_recv.at[frm], frm,
        )
        copy.wait_send()
        copy.wait_recv()
        return carry

    lax.fori_loop(1, n_seq, dout_arrived, 0)

    def pair_copy(u):
        return remote(
            pair_send.at[u], pair_recv.at[u], pair_ssem.at[u], pair_rsem.at[u], {"sub": 1 - sub}
        )

    def pair_out(u):
        pair_copy(u).wait()
        for part in range(2):
            order = 2 * u + part
            at = rows_of(order, sub)
            for t, total in enumerate((dkeys, dvalues)):
                pair_sum[u, t, part] = (total[at, :] + pair_recv[u, t, part].astype(F32)).astype(BF16)
                give(DK + t, pair_sum.at[u, t, part], order)

    mid_copy = remote(mid_mine, mid_theirs, swap_send.at[2], swap_recv.at[2], {"head": 1 - head})

    def lora_middle():
        settle(LOOK)
        mid_mine[...] = dot_nt(down_ref[...], attn_full[...])
        mid_copy.start()

    def peer_id(p):
        return {"seq": p // 2, "sub": lax.rem(p, 2)}

    def lora_parts():
        mid_copy.wait()
        middle = mid_mine[...] + mid_theirs[...]
        up_part = 2.0 * folded(dot_nn(three_terms(middle), g_all[head]))
        down_part = 2.0 * folded(dot_nn(three_terms(upward[...]), attn_full[...]))
        stack = jnp.concatenate((down_part, up_part[:, :feats], up_part[:, feats:]), axis=0)
        half = stack.shape[0] // 2
        for c in range(n_seq):
            pieces[c] = stack[:half, c * HD : (c + 1) * HD]
            pieces[n_seq + c] = stack[half:, c * HD : (c + 1) * HD]
        gathered[mine] = pieces[mine]

        def one(n, carry):
            p = lax.rem(mine + n, peers)
            remote(
                pieces.at[p], gathered.at[mine], rs_send.at[p], rs_recv.at[mine], peer_id(p)
            ).start()
            return carry

        lax.fori_loop(1, peers, one, 0)

    def lora_total():
        def one(n, carry):
            p = lax.rem(mine + n, peers)
            copy = remote(pieces.at[p], gathered.at[p], rs_send.at[p], rs_recv.at[p], peer_id(p))
            copy.wait_send()
            copy.wait_recv()
            return carry

        lax.fori_loop(1, peers, one, 0)
        totals[mine] = jnp.sum(gathered[...], axis=0)

        def share(n, carry):
            p = lax.rem(mine + n, peers)
            remote(
                totals.at[mine], totals.at[mine], ag_send.at[p], ag_recv.at[mine], peer_id(p)
            ).start()
            return carry

        lax.fori_loop(1, peers, share, 0)

    def lora_end():
        def one(n, carry):
            p = lax.rem(mine + n, peers)
            remote(totals.at[mine], totals.at[mine], ag_send.at[p], ag_recv.at[mine], peer_id(p)).wait_send()
            remote(totals.at[p], totals.at[p], ag_send.at[p], ag_recv.at[p], peer_id(p)).wait_recv()
            return carry

        lax.fori_loop(1, peers, one, 0)
        over = rank // 2
        for c in range(n_seq):
            at = slice(c * HD, (c + 1) * HD)
            down_out[:, at] = totals[c, :rank, :]
            up_out[:over, at] = totals[c, rank:, :]
            up_out[over:, at] = totals[n_seq + c, :over, :]
            up_out[:, feats + c * HD : feats + (c + 1) * HD] = totals[n_seq + c, over:, :]

    for u in reversed(range(tiles)):
        base, extent = span(u)
        q = queries[u * tile : (u + 1) * tile, :]
        g = douts[u * tile : (u + 1) * tile, :]
        prob = probs[base : base + extent, :]
        dprob = dot_nt(values[:extent, :], g)
        delta = jnp.sum(prob * dprob, axis=0, keepdims=True)
        dscore = (prob * (dprob - delta) * SCALE).astype(BF16)
        dq_send[u * tile : (u + 1) * tile, :] = dot_nn(keys_t[:, :extent], dscore).T.astype(BF16)
        for order in (2 * u, 2 * u + 1):
            give(DQ, dq_send.at[order * HD : (order + 1) * HD, :], order)
        dk = dot_nn(dscore, q)
        dv = dot_nn(prob.astype(BF16), g)
        if u == tiles - 1:
            dkeys[:extent, :] = dk
            dvalues[:extent, :] = dv
        else:
            dkeys[:extent, :] += dk
            dvalues[:extent, :] += dv
        for part in range(2):
            at = rows_of(2 * u + part, 1 - sub)
            pair_send[u, 0, part] = dkeys[at, :].astype(BF16)
            pair_send[u, 1, part] = dvalues[at, :].astype(BF16)
        pair_copy(u).start()
        if u < tiles - 1:
            pair_out(u + 1)
        if u == tiles - 1:
            lora_middle()
        if u == tiles - 2:
            lora_parts()
    pair_out(0)
    lora_total()

    def in_sent(n, carry):
        for t in range(3):
            in_wait(t, ring(n)).wait_send()
        return carry

    lax.fori_loop(1, n_seq, in_sent, 0)
    lora_end()
    for kind in (DQ, DK, DV):
        settle(kind)


def on_device_heads(
    head_query_rows,
    head_key_rows,
    head_value_rows,
    output_gradient,
    output_matrix,
    adapter_down_weight,
    adapter_up_weight,
):
    rows, feats = head_query_rows.shape
    n_seq = feats // HD
    cols = output_gradient.shape[1]
    rank = adapter_up_weight.shape[0]
    total = 2 * n_seq * rows
    tiles = n_seq // 2
    pieces = 3 * rank * feats // (2 * n_seq * HD)
    vmem = pl.BlockSpec(memory_space=pltpu.VMEM)
    anywhere = pl.BlockSpec(memory_space=pl.ANY)
    dma = pltpu.SemaphoreType.DMA
    dq, dk, dv, down, up = pl.pallas_call(
        lambda *refs: whole_kernel(n_seq, *refs),
        out_shape=[jax.ShapeDtypeStruct((rows, feats), BF16)] * 3
        + [jax.ShapeDtypeStruct((rank, feats), F32), jax.ShapeDtypeStruct((rank, cols), F32)],
        in_specs=[anywhere] * 5 + [vmem] * 2,
        out_specs=[anywhere] * 3 + [vmem] * 2,
        scratch_shapes=[
            pltpu.VMEM((2, rows, cols), BF16),
            pltpu.VMEM((2, feats, cols), BF16),
            pltpu.VMEM((total // 2, HD), BF16),
            pltpu.VMEM((total, HD), BF16),
            pltpu.VMEM((total, HD), BF16),
            pltpu.VMEM((total // 2, HD), BF16),
            pltpu.VMEM((n_seq, rows, HD), BF16),
            pltpu.VMEM((HD, total), BF16),
            pltpu.VMEM((HD, total), BF16),
            pltpu.VMEM((tiles * (tiles + 1) * 2 * HD, 2 * HD), F32),
            pltpu.VMEM((total // 2, HD), BF16),
            pltpu.VMEM((total // 2, HD), BF16),
            pltpu.VMEM((rows, feats), BF16),
            pltpu.VMEM((total, HD), F32),
            pltpu.VMEM((total, HD), F32),
            pltpu.VMEM((tiles, 2, 2, rows, HD), BF16),
            pltpu.VMEM((tiles, 2, 2, rows, HD), BF16),
            pltpu.VMEM((tiles, 2, 2, rows, HD), BF16),
            pltpu.VMEM((rank, rows), F32),
            pltpu.VMEM((rank, rows), F32),
            pltpu.VMEM((rank, rows), F32),
            pltpu.VMEM((2 * n_seq, pieces, HD), F32),
            pltpu.VMEM((2 * n_seq, pieces, HD), F32),
            pltpu.VMEM((2 * n_seq, pieces, HD), F32),
            dma((2,)), dma((3,)), dma((3,)),
            dma((3, n_seq)), dma((3, n_seq)), dma((3,)),
            dma((2, n_seq)), dma((2, n_seq)),
            dma((n_seq,)), dma((n_seq,)),
            dma((4, n_seq)), dma((4, n_seq)), dma((4,)),
            dma((tiles,)), dma((tiles,)),
            dma((2 * n_seq,)), dma((2 * n_seq,)), dma((2 * n_seq,)), dma((2 * n_seq,)),
        ],
        compiler_params=pltpu.CompilerParams(
            collective_id=0, has_side_effects=True, vmem_limit_bytes=48 * 1024 * 1024
        ),
    )(
        head_query_rows, head_key_rows, head_value_rows, output_gradient, output_matrix,
        adapter_down_weight.T, adapter_up_weight,
    )
    return dq, dk, dv, down.T, up


def one_group(mesh, rows, feats, width, lora):
    seq, head, sub = mesh.shape["seq"], mesh.shape["head"], mesh.shape["sub"]
    return (
        sub == 2
        and head == 2
        and rows == HD
        and seq % 2 == 0
        and seq * sub * rows == GROUP
        and feats == seq * HD
        and width == 2 * feats
        and lora == 16
    )


def solution(mesh):
    in_specs = (
        P(("rep", "seq", "sub"), "head"),
        P(("rep", "seq", "sub"), "head"),
        P(("rep", "seq", "sub"), "head"),
        P(("rep", "seq", "sub"), "head"),
        P("head", "sub"),
        P("head", None),
        P(),
    )
    out_specs = (
        P(("rep", "seq", "sub"), "head"),
        P(("rep", "seq", "sub"), "head"),
        P(("rep", "seq", "sub"), "head"),
        P(("rep", "head"), None),
        P("rep", "head"),
    )
    def on_device(*local):
        if one_group(mesh, *local[0].shape, local[3].shape[1], local[6].shape[0]):
            return on_device_heads(*local)
        return on_device_windows(*local)

    return jax.shard_map(
        on_device, mesh=mesh, in_specs=in_specs, out_specs=out_specs, check_vma=False
    )
```

```python
import jax
import jax.numpy as jnp
from jax import lax
from jax.experimental import pallas as pl
from jax.experimental.pallas import tpu as pltpu
from jax.sharding import PartitionSpec as P

HD = 128
GROUP = 2048


def passed_along(value, axis, by):
    peers = lax.axis_size(axis)
    return lax.ppermute(value, axis, [(i, (i + by) % peers) for i in range(peers)])


def placed_visible(row_count, window_rows, seq_total, first_row, back_rows, roll_by):
    query_pos = first_row + lax.broadcasted_iota(jnp.int32, (row_count, window_rows), 0)
    key_pos = (
        first_row
        - back_rows
        + seq_total
        + lax.broadcasted_iota(jnp.int32, (row_count, window_rows), 1)
    ) % seq_total
    query_order = (query_pos - roll_by + seq_total) % seq_total
    key_order = (key_pos - roll_by + seq_total) % seq_total
    return (query_order // GROUP == key_order // GROUP) & (key_order <= query_order)


def softmax_rows(query_head, keys_head, visible):
    scores = lax.dot_general(
        query_head, keys_head, (((1,), (1,)), ((), ())), preferred_element_type=jnp.float32
    )
    scores = jnp.where(visible, scores * HD ** (-0.5), -jnp.inf)
    highest = jnp.max(scores, axis=1, keepdims=True)
    powers = jnp.exp(scores - highest)
    return powers / jnp.sum(powers, axis=1, keepdims=True)


def head_forward(query_head, window_head, visible):
    prob = softmax_rows(query_head, window_head[0], visible)
    return jnp.dot(
        prob.astype(jnp.bfloat16), window_head[1], preferred_element_type=jnp.float32
    ).astype(jnp.bfloat16)


def head_backward(query_head, window_head, dout_head, visible):
    prob = softmax_rows(query_head, window_head[0], visible)
    prob_lo = prob.astype(jnp.bfloat16)
    dprob = lax.dot_general(
        dout_head, window_head[1], (((1,), (1,)), ((), ())), preferred_element_type=jnp.float32
    )
    delta = jnp.sum(prob * dprob, axis=1, keepdims=True)
    dscore = (prob * (dprob - delta) * HD ** (-0.5)).astype(jnp.bfloat16)
    grad_q = jnp.dot(dscore, window_head[0], preferred_element_type=jnp.float32).astype(
        jnp.bfloat16
    )
    grad_k = lax.dot_general(
        dscore, query_head, (((0,), (0,)), ((), ())), preferred_element_type=jnp.float32
    )
    grad_v = lax.dot_general(
        prob_lo, dout_head, (((0,), (0,)), ((), ())), preferred_element_type=jnp.float32
    )
    return (grad_q, jnp.stack((grad_k.astype(jnp.bfloat16), grad_v.astype(jnp.bfloat16))))


def attend_window(query_rows, window, dout_rows, visible):
    row_count, feat_count = query_rows.shape
    heads_here = feat_count // HD
    window_rows = window.shape[1]
    window_heads = window.reshape(2, window_rows, heads_here, HD).transpose(2, 0, 1, 3)
    query_heads = query_rows.reshape(row_count, heads_here, HD).transpose(1, 0, 2)
    dout_heads = dout_rows.reshape(row_count, heads_here, HD).transpose(1, 0, 2)
    attn_heads = lax.map(
        lambda pieces: head_forward(pieces[0], pieces[1], visible), (query_heads, window_heads)
    )
    grad_q_heads, pair_heads = lax.map(
        lambda pieces: head_backward(pieces[0], pieces[1], pieces[2], visible),
        (query_heads, window_heads, dout_heads),
    )
    attention_output = attn_heads.transpose(1, 0, 2).reshape(row_count, feat_count)
    query_gradient = grad_q_heads.transpose(1, 0, 2).reshape(row_count, feat_count)
    pair_grads = pair_heads.transpose(1, 2, 0, 3).reshape(2, window_rows, feat_count)
    return (attention_output, query_gradient, pair_grads)


def on_device_windows(
    head_query_rows,
    head_key_rows,
    head_value_rows,
    output_gradient,
    output_matrix,
    adapter_down_weight,
    adapter_up_weight,
):
    tokens_dev, feat_dev = head_query_rows.shape
    head_index = lax.axis_index("head")
    shifted = head_index >= lax.axis_size("head") // 2
    total_gradient = lax.all_gather(output_gradient, "head", axis=1, tiled=True)
    projected_output = lax.dot_general(
        total_gradient,
        lax.all_gather(output_matrix, "sub", axis=1, tiled=True),
        (((1,), (1,)), ((), ())),
        preferred_element_type=jnp.float32,
    )
    adapter_upward = lax.dot_general(
        total_gradient,
        adapter_up_weight,
        (((1,), (1,)), ((), ())),
        preferred_element_type=jnp.float32,
    )
    adapter_backward = jnp.dot(
        adapter_upward, adapter_down_weight.astype(jnp.float32).T, precision=lax.Precision.HIGHEST
    )
    attention_gradient = (projected_output + 2.0 * adapter_backward).astype(jnp.bfloat16)
    sub_count = lax.axis_size("sub")
    block_rows = tokens_dev * sub_count
    seq_total = block_rows * lax.axis_size("seq")
    reach = max(GROUP // block_rows - 1, 1)
    roll_by = jnp.where(shifted, GROUP // 2, 0)
    stacked = jnp.stack((head_query_rows, head_key_rows, head_value_rows, attention_gradient))
    moved = lax.all_to_all(stacked, "sub", split_axis=2, concat_axis=1, tiled=True)
    own_pair = moved[1:3]
    received = [passed_along(own_pair, "seq", distance) for distance in range(reach, 0, -1)]
    window = jnp.concatenate(received + [own_pair], axis=1)
    first_row = lax.axis_index("seq") * block_rows
    visible = placed_visible(
        block_rows, window.shape[1], seq_total, first_row, reach * block_rows, roll_by
    )
    attn_local, grad_q_local, pair_grads = attend_window(moved[0], window, moved[3], visible)
    running = pair_grads[:, reach * block_rows :].astype(jnp.float32)
    for distance in range(1, reach + 1):
        begin_row = (reach - distance) * block_rows
        block_terms = pair_grads[:, begin_row : begin_row + block_rows]
        returned = passed_along(block_terms, "seq", -distance)
        running = running + returned.astype(jnp.float32)
    pair_local = running.astype(jnp.bfloat16)
    back = jnp.stack((attn_local, grad_q_local, pair_local[0], pair_local[1]))
    restored = lax.all_to_all(back, "sub", split_axis=1, concat_axis=2, tiled=True)
    attention_output = restored[0]
    query_gradient = restored[1]
    key_gradient = restored[2]
    value_gradient = restored[3]
    middle_piece = jnp.dot(
        attention_output, adapter_down_weight, preferred_element_type=jnp.float32
    )
    down_gradient_part = 2.0 * jnp.dot(
        attention_output.astype(jnp.float32).T, adapter_upward, precision=lax.Precision.HIGHEST
    )
    adapter_middle = lax.psum(middle_piece, "head")
    up_gradient_part = 2.0 * jnp.dot(
        adapter_middle.T, output_gradient.astype(jnp.float32), precision=lax.Precision.HIGHEST
    )
    adapter_down_gradient, adapter_up_gradient = lax.psum(
        (down_gradient_part, up_gradient_part), ("seq", "sub")
    )
    return (
        query_gradient,
        key_gradient,
        value_gradient,
        adapter_down_gradient,
        adapter_up_gradient,
    )


SCALE = HD ** (-0.5)
LOG2E = 1.4426950408889634
F32, BF16 = jnp.float32, jnp.bfloat16
LOOK, DQ, DK, DV = range(4)


def dot_nn(left, right):
    return lax.dot_general(left, right, (((1,), (0,)), ((), ())), preferred_element_type=F32)


def dot_nt(left, right):
    return lax.dot_general(left, right, (((1,), (1,)), ((), ())), preferred_element_type=F32)


def dot_tn(left, right):
    return lax.dot_general(left, right, (((0,), (0,)), ((), ())), preferred_element_type=F32)


def three_terms(value):
    high = value.astype(BF16)
    rest = value - high.astype(F32)
    mid = rest.astype(BF16)
    low = (rest - mid.astype(F32)).astype(BF16)
    return jnp.concatenate((high, mid, low), axis=0)


def folded(product):
    rank = product.shape[0] // 3
    return product[:rank] + product[rank : 2 * rank] + product[2 * rank :]


def whole_kernel(
    n_seq,
    q_ref, k_ref, v_ref, g_ref, w_ref, down_hbm, up_hbm,
    dq_ref, dk_ref, dv_ref, down_out, up_out,
    down_ref, up_ref, g_all, w_all, queries, keys, values, douts, dout_send,
    keys_t, values_t, probs, attn_send, dq_send, mid_send, mid_parts, up_all, dkeys, dvalues,
    pair_send, pair_recv, pair_sum, upward, mid_mine, mid_theirs, down_mine, down_theirs,
    down_all, pieces, sub_in, halves, gathered, totals, totals_away,
    local_sem, swap_send, swap_recv, in_send, in_recv, in_local, kv_send, kv_recv,
    do_send, do_recv, back_send, back_recv, back_local, pair_ssem, pair_rsem,
    rs_send, rs_recv, ag_send, ag_recv, up_send, up_recv, da_send, da_recv,
):
    me, head, sub = lax.axis_index("seq"), lax.axis_index("head"), lax.axis_index("sub")
    rank = down_ref.shape[0]
    feats = down_ref.shape[1]
    cols = g_ref.shape[1]
    peers = 2 * n_seq
    mine = me * 2 + sub
    first = head * (n_seq // 2)
    own_at = sub * HD

    def step_of(n):
        return 1 + lax.rem(n - 1 + sub * (n_seq // 2 - 1), n_seq - 1)

    def ring(n):
        return lax.rem(me + step_of(n), n_seq)

    def place_of(block):
        return lax.rem(block - first + n_seq, n_seq)

    def rows_of(order, which):
        return pl.ds(pl.multiple_of(order * (2 * HD) + which * HD, HD), HD)

    def own_rows(order):
        return pl.ds(pl.multiple_of(order * HD, HD), HD)

    def lanes(block):
        return pl.ds(pl.multiple_of(block * HD, HD), HD)

    def remote(src, dst, send, recv, device):
        return pltpu.make_async_remote_copy(
            src_ref=src, dst_ref=dst, send_sem=send, recv_sem=recv,
            device_id=device, device_id_type=pl.DeviceIdType.MESH,
        )

    def across(src, dst, send, recv, device):
        return remote(src, dst, send, recv, {"seq": device})

    barrier = pltpu.get_barrier_semaphore()

    def greet(n, carry):
        p = lax.rem(mine + n, peers)
        pl.semaphore_signal(
            barrier, inc=1, device_id={"seq": p // 2, "sub": lax.rem(p, 2)},
            device_id_type=pl.DeviceIdType.MESH,
        )
        return carry

    own_g = pltpu.make_async_copy(g_ref, g_all.at[head], local_sem.at[0])
    own_w = pltpu.make_async_copy(w_ref, w_all.at[sub], local_sem.at[1])
    own_g.start()
    own_w.start()
    own_down = pltpu.make_async_copy(down_hbm, down_ref, local_sem.at[2])
    own_up = pltpu.make_async_copy(up_hbm, up_ref, local_sem.at[3])
    own_down.start()
    own_up.start()
    lax.fori_loop(1, peers, greet, 0)
    pl.semaphore_signal(
        barrier, inc=1, device_id={"head": 1 - head}, device_id_type=pl.DeviceIdType.MESH
    )
    pl.semaphore_wait(barrier, peers)

    g_swap = remote(g_ref, g_all.at[head], swap_send.at[0], swap_recv.at[0], {"head": 1 - head})
    w_swap = remote(w_ref, w_all.at[sub], swap_send.at[1], swap_recv.at[1], {"sub": 1 - sub})
    g_swap.start()
    w_swap.start()

    o_me = place_of(me)

    def inward(n, carry):
        to = ring(n)
        for t, (src, dst, at) in enumerate(
            (
                (k_ref, keys, rows_of(o_me, sub)),
                (v_ref, values, rows_of(o_me, sub)),
                (q_ref, queries, own_rows(o_me)),
            )
        ):
            across(
                src.at[:, lanes(to)], dst.at[at, :], in_send.at[t, to], in_recv.at[t, me], to
            ).start()
        return carry

    lax.fori_loop(1, n_seq, inward, 0)
    own_in = [
        pltpu.make_async_copy(src.at[:, lanes(me)], dst.at[at, :], in_local.at[t])
        for t, (src, dst, at) in enumerate(
            (
                (k_ref, keys, rows_of(o_me, sub)),
                (v_ref, values, rows_of(o_me, sub)),
                (q_ref, queries, own_rows(o_me)),
            )
        )
    ]
    for copy in own_in:
        copy.start()

    own_g.wait()
    own_w.wait()
    own_down.wait()
    own_up.wait()
    g_swap.wait()
    upward[...] = dot_nt(up_ref[:, :cols], g_all[0]) + dot_nt(up_ref[:, cols:], g_all[1])
    up_all[o_me] = upward[...]

    def up_copy(to, at):
        return across(upward, up_all.at[at], up_send.at[to], up_recv.at[at], to)

    def up_out_to(n, carry):
        up_copy(ring(n), o_me).start()
        return carry

    lax.fori_loop(1, n_seq, up_out_to, 0)
    w_swap.wait()
    up_terms = three_terms(upward[...])

    def dout_of(h):
        rows = pl.ds(pl.multiple_of(h * HD, HD), HD)
        projected = dot_nt(g_all[0], w_all[0, rows, :]) + dot_nt(g_all[1], w_all[1, rows, :])
        down = down_ref[:, lanes(h)]
        adapter = dot_tn(up_terms, jnp.concatenate((down, down, down), axis=0))
        return (projected + 2.0 * adapter).astype(BF16)

    def send_dout(n, carry):
        to = ring(n)
        dout_send[to] = dout_of(to)
        across(
            dout_send.at[to], douts.at[own_rows(o_me), :], do_send.at[to], do_recv.at[me], to
        ).start()
        return carry

    for copy in own_in:
        copy.wait()

    def kv_copy(t, order):
        dst = keys if t == 0 else values
        at = rows_of(order, sub)
        return remote(
            dst.at[at, :], dst.at[at, :], kv_send.at[t, order], kv_recv.at[t, order],
            {"sub": 1 - sub},
        )

    def in_wait(t, frm):
        dst, at = (
            (keys, rows_of(place_of(frm), sub)),
            (values, rows_of(place_of(frm), sub)),
            (queries, own_rows(place_of(frm))),
        )[t]
        src = (k_ref, v_ref, q_ref)[t]
        return across(src.at[:, lanes(frm)], dst.at[at, :], in_send.at[t, frm], in_recv.at[t, frm], frm)

    kv_copy(0, o_me).start()
    kv_copy(1, o_me).start()

    def hand_on(n, carry):
        frm = lax.rem(me - step_of(n) + n_seq, n_seq)
        for t in range(2):
            in_wait(t, frm).wait_recv()
            kv_copy(t, place_of(frm)).start()
        in_wait(2, frm).wait_recv()
        return carry

    def both(n, carry):
        send_dout(n, carry)
        return hand_on(n, carry)

    lax.fori_loop(1, n_seq, both, 0)
    douts[own_rows(o_me), :] = dout_of(me)

    def kv_arrived(order, carry):
        for t in range(2):
            dst = keys if t == 0 else values
            at = rows_of(order, 1 - sub)
            remote(
                dst.at[at, :], dst.at[at, :], kv_send.at[t, order], kv_recv.at[t, order],
                {"sub": 1 - sub},
            ).wait_recv()
            kv_copy(t, order).wait_send()
        return carry

    lax.fori_loop(0, n_seq, kv_arrived, 0)
    keys_t[...] = keys[...].T
    values_t[...] = values[...].T

    sinks = (None, dq_ref, dk_ref, dv_ref)

    def sink(kind, who):
        return mid_parts.at[who] if kind == LOOK else sinks[kind].at[:, lanes(who)]

    def give(kind, src, order):
        to = lax.rem(order + first, n_seq)
        dst = sink(kind, me)

        @pl.when(to == me)
        def _():
            pltpu.make_async_copy(src, dst, back_local.at[kind]).start()

        @pl.when(to != me)
        def _():
            across(src, dst, back_send.at[kind, to], back_recv.at[kind, me], to).start()

    def settle(kind):
        src = mid_send.at[0] if kind == LOOK else dq_send.at[own_rows(0), :]
        pltpu.make_async_copy(src, sink(kind, me), back_local.at[kind]).wait()

        def one(n, carry):
            peer = ring(n)
            copy = across(
                src, sink(kind, peer), back_send.at[kind, peer],
                back_recv.at[kind, peer], peer,
            )
            copy.wait_send()
            copy.wait_recv()
            return carry

        lax.fori_loop(1, n_seq, one, 0)

    tile = 2 * HD
    tiles = n_seq // 2

    def span(u):
        return u * (u + 1) * tile, (u + 1) * 2 * tile

    for u in reversed(range(tiles)):
        base, extent = span(u)
        settled = extent - 2 * tile
        q = queries[u * tile : (u + 1) * tile, :]
        scores = dot_nt(keys[:extent, :], q)
        key_at = lax.broadcasted_iota(jnp.int32, (2 * tile, tile), 0)
        row = lax.broadcasted_iota(jnp.int32, (2 * tile, tile), 1)
        query_at = row + jnp.where(row >= HD, HD, 0) + own_at
        edge = jnp.where(key_at <= query_at, scores[settled:, :], -jnp.inf)
        scores = edge if settled == 0 else jnp.concatenate((scores[:settled, :], edge), axis=0)
        powers = jnp.exp2((scores - jnp.max(scores, axis=0, keepdims=True)) * (SCALE * LOG2E))
        prob = powers * (1.0 / jnp.sum(powers, axis=0, keepdims=True))
        probs[base : base + extent, :] = prob
        attn = dot_nn(values_t[:, :extent], prob.astype(BF16)).T.astype(BF16)
        attn_send[u * tile : (u + 1) * tile, :] = attn
        middle = dot_nt(down_ref[:, lanes(me)], attn)
        for part in range(2):
            order = 2 * u + part
            mid_send[order] = middle[:, part * HD : (part + 1) * HD]
            give(LOOK, mid_send.at[order], order)

    def dout_arrived(n, carry):
        frm = ring(n)
        copy = across(
            dout_send.at[frm], douts.at[own_rows(place_of(frm)), :], do_send.at[frm],
            do_recv.at[frm], frm,
        )
        copy.wait_send()
        copy.wait_recv()
        return carry

    lax.fori_loop(1, n_seq, dout_arrived, 0)

    def pair_copy(u):
        return remote(
            pair_send.at[u], pair_recv.at[u], pair_ssem.at[u], pair_rsem.at[u], {"sub": 1 - sub}
        )

    def pair_out(u):
        pair_copy(u).wait()
        for part in range(2):
            order = 2 * u + part
            at = rows_of(order, sub)
            for t, total in enumerate((dkeys, dvalues)):
                pair_sum[u, t, part] = (total[at, :] + pair_recv[u, t, part].astype(F32)).astype(BF16)

    mid_copy = remote(mid_mine, mid_theirs, swap_send.at[2], swap_recv.at[2], {"head": 1 - head})

    down_copy = remote(down_mine, down_theirs, swap_send.at[3], swap_recv.at[3], {"sub": 1 - sub})
    half_copy = remote(
        pieces.at[pl.ds((1 - sub) * n_seq, n_seq)], sub_in, swap_send.at[4], swap_recv.at[4],
        {"sub": 1 - sub},
    )
    away_copy = remote(totals, totals_away, swap_send.at[5], swap_recv.at[5], {"sub": 1 - sub})

    def lora_middle():
        settle(LOOK)
        mid_mine[...] = jnp.sum(mid_parts[...], axis=0)
        mid_copy.start()

        def arrived(n, carry):
            up_copy(ring(n), place_of(ring(n))).wait_send()
            up_copy(ring(n), place_of(ring(n))).wait_recv()
            return carry

        lax.fori_loop(1, n_seq, arrived, 0)
        upper = jnp.concatenate([up_all[order] for order in range(n_seq)], axis=1)
        down_mine[...] = 2.0 * folded(dot_nn(three_terms(upper), attn_send[...]))
        down_copy.start()

    def lora_parts():
        mid_copy.wait()
        middle = mid_mine[...] + mid_theirs[...]
        up_part = 2.0 * folded(dot_nn(three_terms(middle), g_all[head]))
        for c in range(peers):
            pieces[c] = up_part[:, c * HD : (c + 1) * HD]
        half_copy.start()
        down_copy.wait()
        down_all[me] = down_mine[...] + down_theirs[...]

        def one(n, carry):
            to = ring(n)
            across(
                down_all.at[me], down_all.at[me], da_send.at[to], da_recv.at[me], to
            ).start()
            return carry

        lax.fori_loop(1, n_seq, one, 0)

    def rs_copy(to, at):
        return across(halves.at[to], gathered.at[at], rs_send.at[to], rs_recv.at[at], to)

    def lora_spread():
        half_copy.wait()
        halves[...] = pieces[pl.ds(sub * n_seq, n_seq)] + sub_in[...]
        gathered[me] = halves[me]

        def one(n, carry):
            rs_copy(ring(n), me).start()
            return carry

        lax.fori_loop(1, n_seq, one, 0)

    def share_copy(to, at):
        return across(totals.at[at], totals.at[at], ag_send.at[to], ag_recv.at[at], to)

    def lora_total():
        def one(n, carry):
            rs_copy(ring(n), ring(n)).wait_send()
            rs_copy(ring(n), ring(n)).wait_recv()
            return carry

        lax.fori_loop(1, n_seq, one, 0)
        totals[me] = jnp.sum(gathered[...], axis=0)

        def share(n, carry):
            share_copy(ring(n), me).start()
            return carry

        lax.fori_loop(1, n_seq, share, 0)

    def lora_end():
        def one(n, carry):
            peer = ring(n)
            share_copy(peer, me).wait_send()
            share_copy(peer, peer).wait_recv()
            across(down_all.at[me], down_all.at[me], da_send.at[peer], da_recv.at[me], peer).wait_send()
            across(
                down_all.at[peer], down_all.at[peer], da_send.at[peer], da_recv.at[peer], peer
            ).wait_recv()
            return carry

        lax.fori_loop(1, n_seq, one, 0)
        away_copy.start()
        away_copy.wait()
        for c in range(n_seq):
            at = slice(c * HD, (c + 1) * HD)
            down_out[:, at] = down_all[c]
            here, away = totals[c], totals_away[c]
            up_out[:, at] = jnp.where(sub == 0, here, away)
            up_out[:, feats + c * HD : feats + (c + 1) * HD] = jnp.where(sub == 0, away, here)

    for u in reversed(range(tiles)):
        base, extent = span(u)
        q = queries[u * tile : (u + 1) * tile, :]
        g = douts[u * tile : (u + 1) * tile, :]
        prob = probs[base : base + extent, :]
        dprob = dot_nt(values[:extent, :], g)
        delta = jnp.sum(prob * dprob, axis=0, keepdims=True)
        dscore = (prob * (dprob - delta) * SCALE).astype(BF16)
        dq_send[u * tile : (u + 1) * tile, :] = dot_nn(keys_t[:, :extent], dscore).T.astype(BF16)
        dk = dot_nn(dscore, q)
        dv = dot_nn(prob.astype(BF16), g)
        if u == tiles - 1:
            dkeys[:extent, :] = dk
            dvalues[:extent, :] = dv
        else:
            dkeys[:extent, :] += dk
            dvalues[:extent, :] += dv
        for part in range(2):
            at = rows_of(2 * u + part, 1 - sub)
            pair_send[u, 0, part] = dkeys[at, :].astype(BF16)
            pair_send[u, 1, part] = dvalues[at, :].astype(BF16)
        pair_copy(u).start()
        if u < tiles - 1:
            pair_out(u + 1)
        if u == tiles - 1:
            lora_middle()
        if u == tiles - 2:
            lora_parts()
        if u == tiles - 3:
            lora_spread()
        if u == 0:
            lora_total()
    pair_out(0)

    def returned(kind, to):
        order = place_of(to)
        if kind == DQ:
            return dq_send.at[own_rows(order), :]
        return pair_sum.at[order // 2, kind - DK, lax.rem(order, 2)]

    def give_back(n, carry):
        to = ring(n)
        for kind in (DQ, DK, DV):
            across(
                returned(kind, to), sink(kind, me), back_send.at[kind, to],
                back_recv.at[kind, me], to,
            ).start()
        return carry

    lax.fori_loop(1, n_seq, give_back, 0)
    for kind in (DQ, DK, DV):
        pltpu.make_async_copy(returned(kind, me), sink(kind, me), back_local.at[kind]).start()

    def in_sent(n, carry):
        for t in range(3):
            in_wait(t, ring(n)).wait_send()
        return carry

    lax.fori_loop(1, n_seq, in_sent, 0)
    lora_end()
    for kind in (DQ, DK, DV):
        settle(kind)


def on_device_heads(
    head_query_rows,
    head_key_rows,
    head_value_rows,
    output_gradient,
    output_matrix,
    adapter_down_weight,
    adapter_up_weight,
):
    rows, feats = head_query_rows.shape
    n_seq = feats // HD
    cols = output_gradient.shape[1]
    rank = adapter_up_weight.shape[0]
    total = 2 * n_seq * rows
    tiles = n_seq // 2
    vmem = pl.BlockSpec(memory_space=pltpu.VMEM)
    anywhere = pl.BlockSpec(memory_space=pltpu.HBM)
    dma = pltpu.SemaphoreType.DMA
    dq, dk, dv, down, up = pl.pallas_call(
        lambda *refs: whole_kernel(n_seq, *refs),
        out_shape=[jax.ShapeDtypeStruct((rows, feats), BF16)] * 3
        + [jax.ShapeDtypeStruct((rank, feats), F32), jax.ShapeDtypeStruct((rank, cols), F32)],
        in_specs=[anywhere] * 7,
        out_specs=[anywhere] * 3 + [vmem] * 2,
        scratch_shapes=[
            pltpu.VMEM((rank, feats), BF16),
            pltpu.VMEM((rank, 2 * cols), BF16),
            pltpu.VMEM((2, rows, cols), BF16),
            pltpu.VMEM((2, feats, cols), BF16),
            pltpu.VMEM((total // 2, HD), BF16),
            pltpu.VMEM((total, HD), BF16),
            pltpu.VMEM((total, HD), BF16),
            pltpu.VMEM((total // 2, HD), BF16),
            pltpu.VMEM((n_seq, rows, HD), BF16),
            pltpu.VMEM((HD, total), BF16),
            pltpu.VMEM((HD, total), BF16),
            pltpu.VMEM((tiles * (tiles + 1) * 2 * HD, 2 * HD), F32),
            pltpu.VMEM((total // 2, HD), BF16),
            pltpu.VMEM((total // 2, HD), BF16),
            pltpu.VMEM((n_seq, rank, rows), F32),
            pltpu.VMEM((n_seq, rank, rows), F32),
            pltpu.VMEM((n_seq, rank, rows), F32),
            pltpu.VMEM((total, HD), F32),
            pltpu.VMEM((total, HD), F32),
            pltpu.VMEM((tiles, 2, 2, rows, HD), BF16),
            pltpu.VMEM((tiles, 2, 2, rows, HD), BF16),
            pltpu.VMEM((tiles, 2, 2, rows, HD), BF16),
            pltpu.VMEM((rank, rows), F32),
            pltpu.VMEM((rank, rows), F32),
            pltpu.VMEM((rank, rows), F32),
            pltpu.VMEM((rank, HD), F32),
            pltpu.VMEM((rank, HD), F32),
            pltpu.VMEM((n_seq, rank, HD), F32),
            pltpu.VMEM((2 * n_seq, rank, HD), F32),
            pltpu.VMEM((n_seq, rank, HD), F32),
            pltpu.VMEM((n_seq, rank, HD), F32),
            pltpu.VMEM((n_seq, rank, HD), F32),
            pltpu.VMEM((n_seq, rank, HD), F32),
            pltpu.VMEM((n_seq, rank, HD), F32),
            dma((4,)), dma((6,)), dma((6,)),
            dma((3, n_seq)), dma((3, n_seq)), dma((3,)),
            dma((2, n_seq)), dma((2, n_seq)),
            dma((n_seq,)), dma((n_seq,)),
            dma((4, n_seq)), dma((4, n_seq)), dma((4,)),
            dma((tiles,)), dma((tiles,)),
            dma((n_seq,)), dma((n_seq,)), dma((n_seq,)), dma((n_seq,)),
            dma((n_seq,)), dma((n_seq,)), dma((n_seq,)), dma((n_seq,)),
        ],
        compiler_params=pltpu.CompilerParams(
            collective_id=0, has_side_effects=True, vmem_limit_bytes=48 * 1024 * 1024
        ),
    )(
        head_query_rows, head_key_rows, head_value_rows, output_gradient, output_matrix,
        adapter_down_weight.T, adapter_up_weight,
    )
    return dq, dk, dv, down.T, up


def one_group(mesh, rows, feats, width, lora):
    seq, head, sub = mesh.shape["seq"], mesh.shape["head"], mesh.shape["sub"]
    return (
        sub == 2
        and head == 2
        and rows == HD
        and seq % 2 == 0
        and seq * sub * rows == GROUP
        and feats == seq * HD
        and width == 2 * feats
        and lora == 16
        and seq >= 6
    )


def solution(mesh):
    in_specs = (
        P(("rep", "seq", "sub"), "head"),
        P(("rep", "seq", "sub"), "head"),
        P(("rep", "seq", "sub"), "head"),
        P(("rep", "seq", "sub"), "head"),
        P("head", "sub"),
        P("head", None),
        P(),
    )
    out_specs = (
        P(("rep", "seq", "sub"), "head"),
        P(("rep", "seq", "sub"), "head"),
        P(("rep", "seq", "sub"), "head"),
        P(("rep", "head"), None),
        P("rep", "head"),
    )
    def on_device(*local):
        if one_group(mesh, *local[0].shape, local[3].shape[1], local[6].shape[0]):
            return on_device_heads(*local)
        return on_device_windows(*local)

    return jax.shard_map(
        on_device, mesh=mesh, in_specs=in_specs, out_specs=out_specs, check_vma=False
    )
```

```python
import jax
import jax.numpy as jnp
from jax import lax
from jax.experimental import pallas as pl
from jax.experimental.pallas import tpu as pltpu
from jax.sharding import PartitionSpec as P

HD = 128
GROUP = 2048


def passed_along(value, axis, by):
    peers = lax.axis_size(axis)
    return lax.ppermute(value, axis, [(i, (i + by) % peers) for i in range(peers)])


def placed_visible(row_count, window_rows, seq_total, first_row, back_rows, roll_by):
    query_pos = first_row + lax.broadcasted_iota(jnp.int32, (row_count, window_rows), 0)
    key_pos = (
        first_row
        - back_rows
        + seq_total
        + lax.broadcasted_iota(jnp.int32, (row_count, window_rows), 1)
    ) % seq_total
    query_order = (query_pos - roll_by + seq_total) % seq_total
    key_order = (key_pos - roll_by + seq_total) % seq_total
    return (query_order // GROUP == key_order // GROUP) & (key_order <= query_order)


def softmax_rows(query_head, keys_head, visible):
    scores = lax.dot_general(
        query_head, keys_head, (((1,), (1,)), ((), ())), preferred_element_type=jnp.float32
    )
    scores = jnp.where(visible, scores * HD ** (-0.5), -jnp.inf)
    highest = jnp.max(scores, axis=1, keepdims=True)
    powers = jnp.exp(scores - highest)
    return powers / jnp.sum(powers, axis=1, keepdims=True)


def head_forward(query_head, window_head, visible):
    prob = softmax_rows(query_head, window_head[0], visible)
    return jnp.dot(
        prob.astype(jnp.bfloat16), window_head[1], preferred_element_type=jnp.float32
    ).astype(jnp.bfloat16)


def head_backward(query_head, window_head, dout_head, visible):
    prob = softmax_rows(query_head, window_head[0], visible)
    prob_lo = prob.astype(jnp.bfloat16)
    dprob = lax.dot_general(
        dout_head, window_head[1], (((1,), (1,)), ((), ())), preferred_element_type=jnp.float32
    )
    delta = jnp.sum(prob * dprob, axis=1, keepdims=True)
    dscore = (prob * (dprob - delta) * HD ** (-0.5)).astype(jnp.bfloat16)
    grad_q = jnp.dot(dscore, window_head[0], preferred_element_type=jnp.float32).astype(
        jnp.bfloat16
    )
    grad_k = lax.dot_general(
        dscore, query_head, (((0,), (0,)), ((), ())), preferred_element_type=jnp.float32
    )
    grad_v = lax.dot_general(
        prob_lo, dout_head, (((0,), (0,)), ((), ())), preferred_element_type=jnp.float32
    )
    return (grad_q, jnp.stack((grad_k.astype(jnp.bfloat16), grad_v.astype(jnp.bfloat16))))


def attend_window(query_rows, window, dout_rows, visible):
    row_count, feat_count = query_rows.shape
    heads_here = feat_count // HD
    window_rows = window.shape[1]
    window_heads = window.reshape(2, window_rows, heads_here, HD).transpose(2, 0, 1, 3)
    query_heads = query_rows.reshape(row_count, heads_here, HD).transpose(1, 0, 2)
    dout_heads = dout_rows.reshape(row_count, heads_here, HD).transpose(1, 0, 2)
    attn_heads = lax.map(
        lambda pieces: head_forward(pieces[0], pieces[1], visible), (query_heads, window_heads)
    )
    grad_q_heads, pair_heads = lax.map(
        lambda pieces: head_backward(pieces[0], pieces[1], pieces[2], visible),
        (query_heads, window_heads, dout_heads),
    )
    attention_output = attn_heads.transpose(1, 0, 2).reshape(row_count, feat_count)
    query_gradient = grad_q_heads.transpose(1, 0, 2).reshape(row_count, feat_count)
    pair_grads = pair_heads.transpose(1, 2, 0, 3).reshape(2, window_rows, feat_count)
    return (attention_output, query_gradient, pair_grads)


def on_device_windows(
    head_query_rows,
    head_key_rows,
    head_value_rows,
    output_gradient,
    output_matrix,
    adapter_down_weight,
    adapter_up_weight,
):
    tokens_dev, feat_dev = head_query_rows.shape
    head_index = lax.axis_index("head")
    shifted = head_index >= lax.axis_size("head") // 2
    total_gradient = lax.all_gather(output_gradient, "head", axis=1, tiled=True)
    projected_output = lax.dot_general(
        total_gradient,
        lax.all_gather(output_matrix, "sub", axis=1, tiled=True),
        (((1,), (1,)), ((), ())),
        preferred_element_type=jnp.float32,
    )
    adapter_upward = lax.dot_general(
        total_gradient,
        adapter_up_weight,
        (((1,), (1,)), ((), ())),
        preferred_element_type=jnp.float32,
    )
    adapter_backward = jnp.dot(
        adapter_upward, adapter_down_weight.astype(jnp.float32).T, precision=lax.Precision.HIGHEST
    )
    attention_gradient = (projected_output + 2.0 * adapter_backward).astype(jnp.bfloat16)
    sub_count = lax.axis_size("sub")
    block_rows = tokens_dev * sub_count
    seq_total = block_rows * lax.axis_size("seq")
    reach = max(GROUP // block_rows - 1, 1)
    roll_by = jnp.where(shifted, GROUP // 2, 0)
    stacked = jnp.stack((head_query_rows, head_key_rows, head_value_rows, attention_gradient))
    moved = lax.all_to_all(stacked, "sub", split_axis=2, concat_axis=1, tiled=True)
    own_pair = moved[1:3]
    received = [passed_along(own_pair, "seq", distance) for distance in range(reach, 0, -1)]
    window = jnp.concatenate(received + [own_pair], axis=1)
    first_row = lax.axis_index("seq") * block_rows
    visible = placed_visible(
        block_rows, window.shape[1], seq_total, first_row, reach * block_rows, roll_by
    )
    attn_local, grad_q_local, pair_grads = attend_window(moved[0], window, moved[3], visible)
    running = pair_grads[:, reach * block_rows :].astype(jnp.float32)
    for distance in range(1, reach + 1):
        begin_row = (reach - distance) * block_rows
        block_terms = pair_grads[:, begin_row : begin_row + block_rows]
        returned = passed_along(block_terms, "seq", -distance)
        running = running + returned.astype(jnp.float32)
    pair_local = running.astype(jnp.bfloat16)
    back = jnp.stack((attn_local, grad_q_local, pair_local[0], pair_local[1]))
    restored = lax.all_to_all(back, "sub", split_axis=1, concat_axis=2, tiled=True)
    attention_output = restored[0]
    query_gradient = restored[1]
    key_gradient = restored[2]
    value_gradient = restored[3]
    middle_piece = jnp.dot(
        attention_output, adapter_down_weight, preferred_element_type=jnp.float32
    )
    down_gradient_part = 2.0 * jnp.dot(
        attention_output.astype(jnp.float32).T, adapter_upward, precision=lax.Precision.HIGHEST
    )
    adapter_middle = lax.psum(middle_piece, "head")
    up_gradient_part = 2.0 * jnp.dot(
        adapter_middle.T, output_gradient.astype(jnp.float32), precision=lax.Precision.HIGHEST
    )
    adapter_down_gradient, adapter_up_gradient = lax.psum(
        (down_gradient_part, up_gradient_part), ("seq", "sub")
    )
    return (
        query_gradient,
        key_gradient,
        value_gradient,
        adapter_down_gradient,
        adapter_up_gradient,
    )


SCALE = HD ** (-0.5)
LOG2E = 1.4426950408889634
F32, BF16 = jnp.float32, jnp.bfloat16
LOOK, DQ, DK, DV = range(4)


def dot_nn(left, right):
    return lax.dot_general(left, right, (((1,), (0,)), ((), ())), preferred_element_type=F32)


def dot_nt(left, right):
    return lax.dot_general(left, right, (((1,), (1,)), ((), ())), preferred_element_type=F32)


def dot_tn(left, right):
    return lax.dot_general(left, right, (((0,), (0,)), ((), ())), preferred_element_type=F32)


def three_terms(value):
    high = value.astype(BF16)
    rest = value - high.astype(F32)
    mid = rest.astype(BF16)
    low = (rest - mid.astype(F32)).astype(BF16)
    return jnp.concatenate((high, mid, low), axis=0)


def folded(product):
    rank = product.shape[0] // 3
    return product[:rank] + product[rank : 2 * rank] + product[2 * rank :]


def whole_kernel(
    n_seq,
    q_ref, k_ref, v_ref, g_ref, w_ref, down_hbm, up_hbm,
    dq_ref, dk_ref, dv_ref, down_out, up_out,
    down_ref, up_ref, g_all, w_all, queries, keys, values, douts, dout_send,
    keys_t, values_t, probs, attn_send, dq_send, mid_send, mid_parts, up_all, dkeys, dvalues,
    pair_send, pair_recv, pair_sum, upward, mid_mine, mid_theirs, down_mine, down_theirs,
    down_all, pieces, sub_in, halves, gathered, totals, totals_away,
    local_sem, swap_send, swap_recv, in_send, in_recv, in_local, kv_send, kv_recv,
    do_send, do_recv, back_send, back_recv, back_local, pair_ssem, pair_rsem,
    rs_send, rs_recv, ag_send, ag_recv, up_send, up_recv, da_send, da_recv,
):
    me, head, sub = lax.axis_index("seq"), lax.axis_index("head"), lax.axis_index("sub")
    rank = down_ref.shape[0]
    feats = down_ref.shape[1]
    cols = g_ref.shape[1]
    peers = 2 * n_seq
    mine = me * 2 + sub
    first = head * (n_seq // 2)
    own_at = sub * HD

    def step_of(n):
        return 1 + lax.rem(n - 1 + sub * (n_seq // 2 - 1), n_seq - 1)

    def ring(n):
        return lax.rem(me + step_of(n), n_seq)

    def place_of(block):
        return lax.rem(block - first + n_seq, n_seq)

    def rows_of(order, which):
        return pl.ds(pl.multiple_of(order * (2 * HD) + which * HD, HD), HD)

    def own_rows(order):
        return pl.ds(pl.multiple_of(order * HD, HD), HD)

    def lanes(block):
        return pl.ds(pl.multiple_of(block * HD, HD), HD)

    def remote(src, dst, send, recv, device):
        return pltpu.make_async_remote_copy(
            src_ref=src, dst_ref=dst, send_sem=send, recv_sem=recv,
            device_id=device, device_id_type=pl.DeviceIdType.MESH,
        )

    def across(src, dst, send, recv, device):
        return remote(src, dst, send, recv, {"seq": device})

    barrier = pltpu.get_barrier_semaphore()

    def greet(n, carry):
        p = lax.rem(mine + n, peers)
        pl.semaphore_signal(
            barrier, inc=1, device_id={"seq": p // 2, "sub": lax.rem(p, 2)},
            device_id_type=pl.DeviceIdType.MESH,
        )
        return carry

    own_g = pltpu.make_async_copy(g_ref, g_all.at[head], local_sem.at[0])
    own_w = pltpu.make_async_copy(w_ref, w_all.at[sub], local_sem.at[1])
    own_g.start()
    own_w.start()
    own_down = pltpu.make_async_copy(down_hbm, down_ref, local_sem.at[2])
    own_up = pltpu.make_async_copy(up_hbm, up_ref, local_sem.at[3])
    own_down.start()
    own_up.start()
    lax.fori_loop(1, peers, greet, 0)
    pl.semaphore_signal(
        barrier, inc=1, device_id={"head": 1 - head}, device_id_type=pl.DeviceIdType.MESH
    )
    pl.semaphore_wait(barrier, peers)

    g_swap = remote(g_ref, g_all.at[head], swap_send.at[0], swap_recv.at[0], {"head": 1 - head})
    w_swap = remote(w_ref, w_all.at[sub], swap_send.at[1], swap_recv.at[1], {"sub": 1 - sub})
    g_swap.start()
    w_swap.start()

    o_me = place_of(me)

    def inward(n, carry):
        to = ring(n)
        for t, (src, dst, at) in enumerate(
            (
                (k_ref, keys, rows_of(o_me, sub)),
                (v_ref, values, rows_of(o_me, sub)),
                (q_ref, queries, own_rows(o_me)),
            )
        ):
            across(
                src.at[:, lanes(to)], dst.at[at, :], in_send.at[t, to], in_recv.at[t, me], to
            ).start()
        return carry

    lax.fori_loop(1, n_seq, inward, 0)
    own_in = [
        pltpu.make_async_copy(src.at[:, lanes(me)], dst.at[at, :], in_local.at[t])
        for t, (src, dst, at) in enumerate(
            (
                (k_ref, keys, rows_of(o_me, sub)),
                (v_ref, values, rows_of(o_me, sub)),
                (q_ref, queries, own_rows(o_me)),
            )
        )
    ]
    for copy in own_in:
        copy.start()

    own_g.wait()
    own_w.wait()
    own_down.wait()
    own_up.wait()
    g_swap.wait()
    upward[...] = dot_nt(up_ref[:, :cols], g_all[0]) + dot_nt(up_ref[:, cols:], g_all[1])
    up_all[o_me] = upward[...]

    def up_copy(to, at):
        return across(upward, up_all.at[at], up_send.at[to], up_recv.at[at], to)

    def up_out_to(n, carry):
        up_copy(ring(n), o_me).start()
        return carry

    lax.fori_loop(1, n_seq, up_out_to, 0)
    w_swap.wait()
    up_terms = three_terms(upward[...])

    def dout_of(h):
        rows = pl.ds(pl.multiple_of(h * HD, HD), HD)
        projected = dot_nt(g_all[0], w_all[0, rows, :]) + dot_nt(g_all[1], w_all[1, rows, :])
        down = down_ref[:, lanes(h)]
        adapter = dot_tn(up_terms, jnp.concatenate((down, down, down), axis=0))
        return (projected + 2.0 * adapter).astype(BF16)

    def send_dout(n, carry):
        to = ring(n)
        dout_send[to] = dout_of(to)
        across(
            dout_send.at[to], douts.at[own_rows(o_me), :], do_send.at[to], do_recv.at[me], to
        ).start()
        return carry

    for copy in own_in:
        copy.wait()

    def kv_copy(t, order):
        dst = keys if t == 0 else values
        at = rows_of(order, sub)
        return remote(
            dst.at[at, :], dst.at[at, :], kv_send.at[t, order], kv_recv.at[t, order],
            {"sub": 1 - sub},
        )

    def in_wait(t, frm):
        dst, at = (
            (keys, rows_of(place_of(frm), sub)),
            (values, rows_of(place_of(frm), sub)),
            (queries, own_rows(place_of(frm))),
        )[t]
        src = (k_ref, v_ref, q_ref)[t]
        return across(src.at[:, lanes(frm)], dst.at[at, :], in_send.at[t, frm], in_recv.at[t, frm], frm)

    kv_copy(0, o_me).start()
    kv_copy(1, o_me).start()

    def hand_on(n, carry):
        frm = lax.rem(me - step_of(n) + n_seq, n_seq)
        for t in range(2):
            in_wait(t, frm).wait_recv()
            kv_copy(t, place_of(frm)).start()
        in_wait(2, frm).wait_recv()
        return carry

    def both(n, carry):
        send_dout(n, carry)
        return hand_on(n, carry)

    lax.fori_loop(1, n_seq, both, 0)
    douts[own_rows(o_me), :] = dout_of(me)

    def kv_arrived(order, carry):
        for t in range(2):
            dst = keys if t == 0 else values
            at = rows_of(order, 1 - sub)
            remote(
                dst.at[at, :], dst.at[at, :], kv_send.at[t, order], kv_recv.at[t, order],
                {"sub": 1 - sub},
            ).wait_recv()
            kv_copy(t, order).wait_send()
        return carry

    lax.fori_loop(0, n_seq, kv_arrived, 0)
    keys_t[...] = keys[...].T
    values_t[...] = values[...].T

    sinks = (None, dq_ref, dk_ref, dv_ref)

    def sink(kind, who):
        return mid_parts.at[who] if kind == LOOK else sinks[kind].at[:, lanes(who)]

    def give(kind, src, order):
        to = lax.rem(order + first, n_seq)
        dst = sink(kind, me)

        @pl.when(to == me)
        def _():
            pltpu.make_async_copy(src, dst, back_local.at[kind]).start()

        @pl.when(to != me)
        def _():
            across(src, dst, back_send.at[kind, to], back_recv.at[kind, me], to).start()

    def settle(kind):
        src = mid_send.at[0] if kind == LOOK else dq_send.at[own_rows(0), :]
        pltpu.make_async_copy(src, sink(kind, me), back_local.at[kind]).wait()

        def one(n, carry):
            peer = ring(n)
            copy = across(
                src, sink(kind, peer), back_send.at[kind, peer],
                back_recv.at[kind, peer], peer,
            )
            copy.wait_send()
            copy.wait_recv()
            return carry

        lax.fori_loop(1, n_seq, one, 0)

    tile = 2 * HD
    tiles = n_seq // 2

    def span(u):
        return u * (u + 1) * tile, (u + 1) * 2 * tile

    for u in reversed(range(tiles)):
        base, extent = span(u)
        settled = extent - 2 * tile
        q = queries[u * tile : (u + 1) * tile, :]
        scores = dot_nt(keys[:extent, :], q)
        key_at = lax.broadcasted_iota(jnp.int32, (2 * tile, tile), 0)
        row = lax.broadcasted_iota(jnp.int32, (2 * tile, tile), 1)
        query_at = row + jnp.where(row >= HD, HD, 0) + own_at
        edge = jnp.where(key_at <= query_at, scores[settled:, :], -jnp.inf)
        scores = edge if settled == 0 else jnp.concatenate((scores[:settled, :], edge), axis=0)
        powers = jnp.exp2((scores - jnp.max(scores, axis=0, keepdims=True)) * (SCALE * LOG2E))
        prob = powers * (1.0 / jnp.sum(powers, axis=0, keepdims=True))
        probs[base : base + extent, :] = prob
        attn = dot_nn(values_t[:, :extent], prob.astype(BF16)).T.astype(BF16)
        attn_send[u * tile : (u + 1) * tile, :] = attn
        middle = dot_nt(down_ref[:, lanes(me)], attn)
        for part in range(2):
            order = 2 * u + part
            mid_send[order] = middle[:, part * HD : (part + 1) * HD]
            give(LOOK, mid_send.at[order], order)

    def dout_arrived(n, carry):
        frm = ring(n)
        copy = across(
            dout_send.at[frm], douts.at[own_rows(place_of(frm)), :], do_send.at[frm],
            do_recv.at[frm], frm,
        )
        copy.wait_send()
        copy.wait_recv()
        return carry

    lax.fori_loop(1, n_seq, dout_arrived, 0)

    def pair_copy(u):
        return remote(
            pair_send.at[u], pair_recv.at[u], pair_ssem.at[u], pair_rsem.at[u], {"sub": 1 - sub}
        )

    def pair_out(u):
        pair_copy(u).wait()
        for part in range(2):
            order = 2 * u + part
            at = rows_of(order, sub)
            for t, total in enumerate((dkeys, dvalues)):
                pair_sum[u, t, part] = (total[at, :] + pair_recv[u, t, part].astype(F32)).astype(BF16)

    mid_copy = remote(mid_mine, mid_theirs, swap_send.at[2], swap_recv.at[2], {"head": 1 - head})

    down_copy = remote(down_mine, down_theirs, swap_send.at[3], swap_recv.at[3], {"sub": 1 - sub})
    half_copy = remote(
        pieces.at[pl.ds((1 - sub) * n_seq, n_seq)], sub_in, swap_send.at[4], swap_recv.at[4],
        {"sub": 1 - sub},
    )
    away_copy = remote(totals, totals_away, swap_send.at[5], swap_recv.at[5], {"sub": 1 - sub})

    def lora_middle():
        settle(LOOK)
        mid_mine[...] = jnp.sum(mid_parts[...], axis=0)
        mid_copy.start()

        def arrived(n, carry):
            up_copy(ring(n), place_of(ring(n))).wait_send()
            up_copy(ring(n), place_of(ring(n))).wait_recv()
            return carry

        lax.fori_loop(1, n_seq, arrived, 0)
        upper = jnp.concatenate([up_all[order] for order in range(n_seq)], axis=1)
        down_mine[...] = 2.0 * folded(dot_nn(three_terms(upper), attn_send[...]))
        down_copy.start()

    def lora_parts():
        mid_copy.wait()
        middle = mid_mine[...] + mid_theirs[...]
        up_part = 2.0 * folded(dot_nn(three_terms(middle), g_all[head]))
        for c in range(peers):
            pieces[c] = up_part[:, c * HD : (c + 1) * HD]
        half_copy.start()
        down_copy.wait()
        down_all[me] = down_mine[...] + down_theirs[...]

        def one(n, carry):
            to = ring(n)
            across(
                down_all.at[me], down_all.at[me], da_send.at[to], da_recv.at[me], to
            ).start()
            return carry

        lax.fori_loop(1, n_seq, one, 0)

    def rs_copy(to, at):
        return across(halves.at[to], gathered.at[at], rs_send.at[to], rs_recv.at[at], to)

    def lora_spread():
        half_copy.wait()
        halves[...] = pieces[pl.ds(sub * n_seq, n_seq)] + sub_in[...]
        gathered[me] = halves[me]

        def one(n, carry):
            rs_copy(ring(n), me).start()
            return carry

        lax.fori_loop(1, n_seq, one, 0)

    def share_copy(to, at):
        return across(totals.at[at], totals.at[at], ag_send.at[to], ag_recv.at[at], to)

    def lora_total():
        def one(n, carry):
            rs_copy(ring(n), ring(n)).wait_send()
            rs_copy(ring(n), ring(n)).wait_recv()
            return carry

        lax.fori_loop(1, n_seq, one, 0)
        totals[me] = jnp.sum(gathered[...], axis=0)

        def share(n, carry):
            share_copy(ring(n), me).start()
            return carry

        lax.fori_loop(1, n_seq, share, 0)

    def lora_end():
        def one(n, carry):
            peer = ring(n)
            share_copy(peer, me).wait_send()
            share_copy(peer, peer).wait_recv()
            across(down_all.at[me], down_all.at[me], da_send.at[peer], da_recv.at[me], peer).wait_send()
            across(
                down_all.at[peer], down_all.at[peer], da_send.at[peer], da_recv.at[peer], peer
            ).wait_recv()
            return carry

        lax.fori_loop(1, n_seq, one, 0)
        away_copy.start()
        away_copy.wait()
        for c in range(n_seq):
            at = slice(c * HD, (c + 1) * HD)
            down_out[:, at] = down_all[c]
            here, away = totals[c], totals_away[c]
            up_out[:, at] = jnp.where(sub == 0, here, away)
            up_out[:, feats + c * HD : feats + (c + 1) * HD] = jnp.where(sub == 0, away, here)

    for u in reversed(range(tiles)):
        base, extent = span(u)
        q = queries[u * tile : (u + 1) * tile, :]
        g = douts[u * tile : (u + 1) * tile, :]
        prob = probs[base : base + extent, :]
        dprob = dot_nt(values[:extent, :], g)
        delta = jnp.sum(prob * dprob, axis=0, keepdims=True)
        dscore = (prob * (dprob - delta) * SCALE).astype(BF16)
        dq_send[u * tile : (u + 1) * tile, :] = dot_nn(keys_t[:, :extent], dscore).T.astype(BF16)
        dk = dot_nn(dscore, q)
        dv = dot_nn(prob.astype(BF16), g)
        if u == tiles - 1:
            dkeys[:extent, :] = dk
            dvalues[:extent, :] = dv
        else:
            dkeys[:extent, :] += dk
            dvalues[:extent, :] += dv
        for part in range(2):
            at = rows_of(2 * u + part, 1 - sub)
            pair_send[u, 0, part] = dkeys[at, :].astype(BF16)
            pair_send[u, 1, part] = dvalues[at, :].astype(BF16)
        pair_copy(u).start()
        if u < tiles - 1:
            pair_out(u + 1)
        if u == tiles - 1:
            lora_middle()
        if u == tiles - 2:
            lora_parts()
        if u == tiles - 3:
            lora_spread()
        if u == 0:
            lora_total()
    def returned(kind, to):
        order = place_of(to)
        if kind == DQ:
            return dq_send.at[own_rows(order), :]
        return pair_sum.at[order // 2, kind - DK, lax.rem(order, 2)]

    def give_queries(n, carry):
        to = ring(n)
        for kind in (DQ,):
            across(
                returned(kind, to), sink(kind, me), back_send.at[kind, to],
                back_recv.at[kind, me], to,
            ).start()
        return carry

    lax.fori_loop(1, n_seq, give_queries, 0)
    pair_out(0)

    def give_back(n, carry):
        to = ring(n)
        for kind in (DK, DV):
            across(
                returned(kind, to), sink(kind, me), back_send.at[kind, to],
                back_recv.at[kind, me], to,
            ).start()
        return carry

    lax.fori_loop(1, n_seq, give_back, 0)
    for kind in (DQ, DK, DV):
        pltpu.make_async_copy(returned(kind, me), sink(kind, me), back_local.at[kind]).start()

    def in_sent(n, carry):
        for t in range(3):
            in_wait(t, ring(n)).wait_send()
        return carry

    lax.fori_loop(1, n_seq, in_sent, 0)
    lora_end()
    for kind in (DQ, DK, DV):
        settle(kind)


def on_device_heads(
    head_query_rows,
    head_key_rows,
    head_value_rows,
    output_gradient,
    output_matrix,
    adapter_down_weight,
    adapter_up_weight,
):
    rows, feats = head_query_rows.shape
    n_seq = feats // HD
    cols = output_gradient.shape[1]
    rank = adapter_up_weight.shape[0]
    total = 2 * n_seq * rows
    tiles = n_seq // 2
    vmem = pl.BlockSpec(memory_space=pltpu.VMEM)
    anywhere = pl.BlockSpec(memory_space=pltpu.HBM)
    dma = pltpu.SemaphoreType.DMA
    dq, dk, dv, down, up = pl.pallas_call(
        lambda *refs: whole_kernel(n_seq, *refs),
        out_shape=[jax.ShapeDtypeStruct((rows, feats), BF16)] * 3
        + [jax.ShapeDtypeStruct((rank, feats), F32), jax.ShapeDtypeStruct((rank, cols), F32)],
        in_specs=[anywhere] * 7,
        out_specs=[anywhere] * 3 + [vmem] * 2,
        scratch_shapes=[
            pltpu.VMEM((rank, feats), BF16),
            pltpu.VMEM((rank, 2 * cols), BF16),
            pltpu.VMEM((2, rows, cols), BF16),
            pltpu.VMEM((2, feats, cols), BF16),
            pltpu.VMEM((total // 2, HD), BF16),
            pltpu.VMEM((total, HD), BF16),
            pltpu.VMEM((total, HD), BF16),
            pltpu.VMEM((total // 2, HD), BF16),
            pltpu.VMEM((n_seq, rows, HD), BF16),
            pltpu.VMEM((HD, total), BF16),
            pltpu.VMEM((HD, total), BF16),
            pltpu.VMEM((tiles * (tiles + 1) * 2 * HD, 2 * HD), F32),
            pltpu.VMEM((total // 2, HD), BF16),
            pltpu.VMEM((total // 2, HD), BF16),
            pltpu.VMEM((n_seq, rank, rows), F32),
            pltpu.VMEM((n_seq, rank, rows), F32),
            pltpu.VMEM((n_seq, rank, rows), F32),
            pltpu.VMEM((total, HD), F32),
            pltpu.VMEM((total, HD), F32),
            pltpu.VMEM((tiles, 2, 2, rows, HD), BF16),
            pltpu.VMEM((tiles, 2, 2, rows, HD), BF16),
            pltpu.VMEM((tiles, 2, 2, rows, HD), BF16),
            pltpu.VMEM((rank, rows), F32),
            pltpu.VMEM((rank, rows), F32),
            pltpu.VMEM((rank, rows), F32),
            pltpu.VMEM((rank, HD), F32),
            pltpu.VMEM((rank, HD), F32),
            pltpu.VMEM((n_seq, rank, HD), F32),
            pltpu.VMEM((2 * n_seq, rank, HD), F32),
            pltpu.VMEM((n_seq, rank, HD), F32),
            pltpu.VMEM((n_seq, rank, HD), F32),
            pltpu.VMEM((n_seq, rank, HD), F32),
            pltpu.VMEM((n_seq, rank, HD), F32),
            pltpu.VMEM((n_seq, rank, HD), F32),
            dma((4,)), dma((6,)), dma((6,)),
            dma((3, n_seq)), dma((3, n_seq)), dma((3,)),
            dma((2, n_seq)), dma((2, n_seq)),
            dma((n_seq,)), dma((n_seq,)),
            dma((4, n_seq)), dma((4, n_seq)), dma((4,)),
            dma((tiles,)), dma((tiles,)),
            dma((n_seq,)), dma((n_seq,)), dma((n_seq,)), dma((n_seq,)),
            dma((n_seq,)), dma((n_seq,)), dma((n_seq,)), dma((n_seq,)),
        ],
        compiler_params=pltpu.CompilerParams(
            collective_id=0, has_side_effects=True, vmem_limit_bytes=48 * 1024 * 1024
        ),
    )(
        head_query_rows, head_key_rows, head_value_rows, output_gradient, output_matrix,
        adapter_down_weight.T, adapter_up_weight,
    )
    return dq, dk, dv, down.T, up


def one_group(mesh, rows, feats, width, lora):
    seq, head, sub = mesh.shape["seq"], mesh.shape["head"], mesh.shape["sub"]
    return (
        sub == 2
        and head == 2
        and rows == HD
        and seq % 2 == 0
        and seq * sub * rows == GROUP
        and feats == seq * HD
        and width == 2 * feats
        and lora == 16
        and seq >= 6
    )


def solution(mesh):
    in_specs = (
        P(("rep", "seq", "sub"), "head"),
        P(("rep", "seq", "sub"), "head"),
        P(("rep", "seq", "sub"), "head"),
        P(("rep", "seq", "sub"), "head"),
        P("head", "sub"),
        P("head", None),
        P(),
    )
    out_specs = (
        P(("rep", "seq", "sub"), "head"),
        P(("rep", "seq", "sub"), "head"),
        P(("rep", "seq", "sub"), "head"),
        P(("rep", "head"), None),
        P("rep", "head"),
    )
    def on_device(*local):
        if one_group(mesh, *local[0].shape, local[3].shape[1], local[6].shape[0]):
            return on_device_heads(*local)
        return on_device_windows(*local)

    return jax.shard_map(
        on_device, mesh=mesh, in_specs=in_specs, out_specs=out_specs, check_vma=False
    )
```
